32 devices in a mesh: wide: 8 (over y, x, core), group: 4 (over z).
Axes of the slice: x: 2, y: 2, z: 4, core: 2. Of those that a mesh axis runs over, the one named last changes fastest.
Arguments:
- inputs: bfloat16 [32, 128, 576], P(('wide', 'group')), may hold values from -6 to 6
- segments: int32 [32, 128], P(('wide', 'group')), may hold values from 0 to 5, never falling along the last dimension, each value on 1 to 64 neighbouring positions
- cotangent: bfloat16 [32, 128, 576], P(('wide', 'group')), may hold values from -6 to 6
- params: float32 [3540096], P('group')
- moment_one: float32 [3540096], P('group')
- moment_two: float32 [3540096], P('group')
Outputs:
- outputs: bfloat16 [32, 128, 576], P(('wide', 'group'))
- d_inputs: bfloat16 [32, 128, 576], P(('wide', 'group'))
- grads: float32 [3540096], P('group')
- new_params: float32 [3540096], P('group')
- new_moment_one: float32 [3540096], P('group')
- new_moment_two: float32 [3540096], P('group')
The draws below stay inside these ranges and needn't reach their ends.
All inputs are finite; a program needn't handle non-finite values.
Results may differ from the reference program's by a relative error of at most 0.023.
Values may be sent and summed in bfloat16 or wider, within the bound.
A program may use at most 128 MiB of HBM per device.

```python
import math
import jax
import jax.numpy as jnp
import numpy as np
from jax import lax

MODEL_WIDTH = 576
QUERY_HEADS = 9
KEY_VALUE_HEADS = 3
HEAD_SIZE = 64
FF = 1536
LEN = 128
SEGS = 6
SEG_MOST = 64
ROWS = 32
NPARAM = 3540096


def draw_params(key, part):
    query_key_value_width = (QUERY_HEADS + 2 * KEY_VALUE_HEADS) * HEAD_SIZE
    streams = jax.random.split(key, 6)
    query_key_value_weight = jax.random.normal(streams[0], (MODEL_WIDTH, query_key_value_width), jnp.float32) * MODEL_WIDTH ** (-0.5)
    output_weight = jax.random.normal(streams[1], (QUERY_HEADS * HEAD_SIZE, MODEL_WIDTH), jnp.float32) * (MODEL_WIDTH / 8.0) ** (-0.5)
    w_gateup = jax.random.normal(streams[2], (MODEL_WIDTH, 2 * FF), jnp.float32) * MODEL_WIDTH ** (-0.5)
    w_down = jax.random.normal(streams[3], (FF, MODEL_WIDTH), jnp.float32) * FF ** (-0.5)
    rising = jnp.exp(jnp.linspace(jnp.log(0.6), jnp.log(1.8), MODEL_WIDTH)).astype(jnp.float32)
    gain_attn = rising * jax.random.uniform(streams[4], (MODEL_WIDTH,), jnp.float32, 0.8, 1.2)
    gain_ffn = rising * jax.random.uniform(streams[5], (MODEL_WIDTH,), jnp.float32, 0.8, 1.2)
    return jnp.concatenate([query_key_value_weight.reshape(-1), output_weight.reshape(-1), w_gateup.reshape(-1), w_down.reshape(-1), gain_attn, gain_ffn]).astype(jnp.float32)


def draw_moment_one(key, part):
    value_rows = jax.random.normal(key, (NPARAM,), jnp.float32) * 0.3
    return (value_rows * NPARAM ** (-0.5)).astype(jnp.float32)


def draw_moment_two(key, part):
    value_rows = jnp.exp(jax.random.uniform(key, (NPARAM,), jnp.float32, jnp.log(0.01), jnp.log(0.1)))
    return (value_rows / NPARAM).astype(jnp.float32)


def levels(key, dims, cuts, least, top_value):
    def one(dim, parts):
        draws = jax.random.uniform(jax.random.fold_in(jax.random.fold_in(key, 6), dim), (parts,), jnp.float32, least / len(cuts), top_value / len(cuts))
        return jnp.repeat(jnp.exp(draws), dims[dim] // parts).reshape((-1,) + (1,) * (len(dims) - dim - 1))

    loudness = one(*cuts[0])
    for cut in cuts[1:]:
        loudness = loudness * one(*cut)
    return loudness


def length_profile(count, total, reach, lean):
    portions = [(1 << 20) // math.isqrt(rank ** lean) + 1 for rank in range(2, count + 1)]
    rest, counts = total - reach - (count - 1), [1] * (count - 1)
    while rest > 0:
        movable = [i for i in range(count - 1) if counts[i] < reach]
        mass, left = sum([portions[i] for i in movable]), rest
        for i in movable:
            addition = min(reach - counts[i], max(1, left * portions[i] // mass), rest)
            counts[i] = counts[i] + addition
            rest = rest - addition
    return np.array([reach] + counts)


def ragged(rng, amount, total, bound, skew):
    if amount == 2:
        one = jax.random.randint(rng, (), max(1, total - bound), min(bound, total - 1) + 1)
        return jnp.stack([one, total - one])
    tallies = jnp.asarray(length_profile(amount, total, bound, skew), jnp.int32)
    couples = (amount - 1) // 2
    source_of, sink = tallies[1:1 + 2 * couples:2], tallies[2:2 + 2 * couples:2]
    margin = jnp.minimum(source_of - 1, bound - sink)
    moved = jax.random.randint(jax.random.fold_in(rng, 1), (couples,), 0, 1 << 20) % (margin + 1)
    tallies = tallies.at[1:1 + 2 * couples:2].set(source_of - moved).at[2:2 + 2 * couples:2].set(sink + moved)
    return tallies[jax.random.permutation(jax.random.fold_in(rng, 2), amount)]


def normal_values(own_key, dims, deviation, most, shards=(), kind=jnp.bfloat16):
    level = levels(own_key, dims, shards, -0.22, 0.18) if shards else 1.0
    drawn = jax.random.normal(own_key, dims, jnp.float32) * deviation * level
    return jnp.minimum(jnp.maximum(drawn, -most), most).astype(kind)


def setup_inputs(seed: int = 0) -> dict:
    seeds = jax.random.split(jax.random.key(seed), 7)
    inputs = normal_values(seeds[0], (ROWS, LEN, MODEL_WIDTH), 1.0, 6.0, ((0, 32),))
    segments = jax.vmap(lambda own: jnp.searchsorted(jnp.cumsum(ragged(own, SEGS, LEN, SEG_MOST, 1)), jnp.arange(LEN), side="right"))(jax.random.split(seeds[1], ROWS)).reshape((ROWS, LEN)).astype(jnp.int32)
    cotangent = normal_values(seeds[2], (ROWS, LEN, MODEL_WIDTH), 1.0, 6.0, ((0, 32),))
    params = draw_params(jax.random.fold_in(seeds[6], 71), 0)
    moment_one = draw_moment_one(jax.random.fold_in(seeds[6], 71), 0)
    moment_two = draw_moment_two(jax.random.fold_in(seeds[6], 71), 0)
    return {"inputs": inputs, "segments": segments, "cotangent": cotangent, "params": params, "moment_one": moment_one, "moment_two": moment_two}


norm_eps = 1e-05
theta_base = 10000.0
masked_value = -1e+30
beta_one = 0.9
beta_two = 0.95
bias_one = 0.19
bias_two = 0.0975
learn_rate = 0.03
decay_rate = 0.1
adam_eps = 1e-08
max_norm = 1.0

def contract(pattern, left_op, right_op):
    return jnp.einsum(pattern, left_op.astype(jnp.float32), right_op.astype(jnp.float32))

def inner_rows(left_op, right_op):
    return lax.dot_general(left_op.astype(jnp.float32), right_op.astype(jnp.float32), (((0,), (0,)), ((), ())))

def outer_column_count(left_op, right_op):
    return lax.dot_general(left_op.astype(jnp.float32), right_op.astype(jnp.float32), (((1,), (1,)), ((), ())))

def unpack(flat):
    query_key_value_width = (QUERY_HEADS + 2 * KEY_VALUE_HEADS) * HEAD_SIZE
    shapes = [(MODEL_WIDTH, query_key_value_width), (QUERY_HEADS * HEAD_SIZE, MODEL_WIDTH), (MODEL_WIDTH, 2 * FF), (FF, MODEL_WIDTH), (MODEL_WIDTH,), (MODEL_WIDTH,)]
    pieces = []
    offset = 0
    for piece_shape in shapes:
        extent = math.prod(piece_shape)
        pieces.append(flat[offset:offset + extent].reshape(piece_shape))
        offset += extent
    return pieces

def positions_of(segment_row):
    index_row = jnp.arange(segment_row.shape[0], dtype=jnp.int32)
    previous = jnp.concatenate([segment_row[:1] - 1, segment_row[:-1]])
    starts = jnp.where(segment_row != previous, index_row, jnp.zeros_like(index_row))
    return index_row - lax.cummax(starts, axis=0)

def rope_tables(positions):
    half_size = HEAD_SIZE // 2
    freqs = theta_base ** (-2.0 * jnp.arange(half_size, dtype=jnp.float32) / HEAD_SIZE)
    angles = positions.astype(jnp.float32)[:, None] * freqs[None, :]
    return (jnp.cos(angles)[:, None, :], jnp.sin(angles)[:, None, :])

def apply_rotation(vectors, cosine_lookup, sine_lookup):
    half_size = HEAD_SIZE // 2
    first_half = vectors[..., :half_size]
    second_half = vectors[..., half_size:]
    return jnp.concatenate([first_half * cosine_lookup - second_half * sine_lookup, second_half * cosine_lookup + first_half * sine_lookup], axis=-1)

def unrotate(vectors, cosine_lookup, sine_lookup):
    half_size = HEAD_SIZE // 2
    first_half = vectors[..., :half_size]
    second_half = vectors[..., half_size:]
    return jnp.concatenate([first_half * cosine_lookup + second_half * sine_lookup, second_half * cosine_lookup - first_half * sine_lookup], axis=-1)

def norm_back(d_hidden, normed, inverse, gain):
    d_normed = d_hidden * gain
    return inverse * (d_normed - normed * lax.optimization_barrier(jnp.mean(d_normed * normed, axis=-1, keepdims=True)))

def layer_row(inputs, segment_row, cotangent, weights):
    query_key_value_weight, output_weight, w_gateup, w_down, gain_attn, gain_ffn = weights
    sequence_length = inputs.shape[0]
    repeat_count = QUERY_HEADS // KEY_VALUE_HEADS
    scale_factor = HEAD_SIZE ** (-0.5)
    gain_one = gain_attn.astype(jnp.float32)
    gain_two = gain_ffn.astype(jnp.float32)
    resid_in = inputs.astype(jnp.float32)
    inv_attn = lax.rsqrt(lax.optimization_barrier(jnp.mean(resid_in * resid_in, axis=-1, keepdims=True)) + norm_eps)
    normed_attn = resid_in * inv_attn
    hidden_attn = (normed_attn * gain_one).astype(jnp.bfloat16)
    projected_output = jnp.dot(hidden_attn, query_key_value_weight, preferred_element_type=jnp.float32)
    cosine_lookup, sine_lookup = rope_tables(positions_of(segment_row))
    query_rows = projected_output[:, :QUERY_HEADS * HEAD_SIZE].reshape(sequence_length, QUERY_HEADS, HEAD_SIZE)
    key_matrix = projected_output[:, QUERY_HEADS * HEAD_SIZE:(QUERY_HEADS + KEY_VALUE_HEADS) * HEAD_SIZE].reshape(sequence_length, KEY_VALUE_HEADS, HEAD_SIZE)
    query_rows_rotated = apply_rotation(query_rows, cosine_lookup, sine_lookup).astype(jnp.bfloat16).reshape(sequence_length, KEY_VALUE_HEADS, repeat_count, HEAD_SIZE)
    keys_rot = apply_rotation(key_matrix, cosine_lookup, sine_lookup).astype(jnp.bfloat16)
    value_rows = projected_output[:, (QUERY_HEADS + KEY_VALUE_HEADS) * HEAD_SIZE:].reshape(sequence_length, KEY_VALUE_HEADS, HEAD_SIZE).astype(jnp.bfloat16)
    index_row = jnp.arange(sequence_length)
    allowed = (segment_row[:, None] == segment_row[None, :]) & (index_row[:, None] >= index_row[None, :])
    scores = contract('qgrd,kgd->grqk', query_rows_rotated, keys_rot) * scale_factor
    scores = jnp.where(allowed, scores, masked_value)
    peak = lax.optimization_barrier(jnp.max(scores, axis=-1, keepdims=True))
    log_total = peak + jnp.log(lax.optimization_barrier(jnp.sum(jnp.exp(scores - peak), axis=-1, keepdims=True)))
    probs = jnp.exp(scores - log_total)
    probs_b = probs.astype(jnp.bfloat16)
    attended = contract('grqk,kgd->qgrd', probs_b, value_rows).astype(jnp.bfloat16).reshape(sequence_length, QUERY_HEADS * HEAD_SIZE)
    mid = resid_in + jnp.dot(attended, output_weight, preferred_element_type=jnp.float32)
    inv_ffn = lax.rsqrt(lax.optimization_barrier(jnp.mean(mid * mid, axis=-1, keepdims=True)) + norm_eps)
    normed_ffn = mid * inv_ffn
    hidden_ffn = (normed_ffn * gain_two).astype(jnp.bfloat16)
    gate_up = jnp.dot(hidden_ffn, w_gateup, preferred_element_type=jnp.float32)
    gate_pre = gate_up[:, :FF]
    upper = gate_up[:, FF:]
    sigmoid_gate = jax.nn.sigmoid(gate_pre)
    activation = (gate_pre * sigmoid_gate * upper).astype(jnp.bfloat16)
    outputs = (mid + jnp.dot(activation, w_down, preferred_element_type=jnp.float32)).astype(jnp.bfloat16)
    grad_down = inner_rows(activation, cotangent)
    d_act = outer_column_count(cotangent, w_down)
    d_gate = d_act * upper * sigmoid_gate * (1.0 + gate_pre * (1.0 - sigmoid_gate))
    d_upper = d_act * gate_pre * sigmoid_gate
    d_gate_up = jnp.concatenate([d_gate, d_upper], axis=-1).astype(jnp.bfloat16)
    grad_gateup = inner_rows(hidden_ffn, d_gate_up)
    d_hidden_ffn = outer_column_count(d_gate_up, w_gateup)
    grad_gain_ffn = lax.optimization_barrier(jnp.sum(d_hidden_ffn * normed_ffn, axis=0))
    d_mid = cotangent.astype(jnp.float32) + norm_back(d_hidden_ffn, normed_ffn, inv_ffn, gain_two)
    grad_middle_batch = d_mid.astype(jnp.bfloat16)
    grad_out = inner_rows(attended, grad_middle_batch)
    grad_attended_rows = outer_column_count(grad_middle_batch, output_weight).astype(jnp.bfloat16).reshape(sequence_length, KEY_VALUE_HEADS, repeat_count, HEAD_SIZE)
    d_probs = contract('qgrd,kgd->grqk', grad_attended_rows, value_rows)
    row_total = lax.optimization_barrier(jnp.sum(probs * d_probs, axis=-1, keepdims=True))
    d_scores = (probs * (d_probs - row_total) * scale_factor).astype(jnp.bfloat16)
    grad_query_rows = contract('grqk,kgd->qgrd', d_scores, keys_rot).reshape(sequence_length, QUERY_HEADS, HEAD_SIZE)
    grad_key_rows = contract('grqk,qgrd->kgd', d_scores, query_rows_rotated)
    grad_value_rows = contract('grqk,qgrd->kgd', probs_b, grad_attended_rows)
    grad_query_rows = unrotate(grad_query_rows, cosine_lookup, sine_lookup)
    grad_key_rows = unrotate(grad_key_rows, cosine_lookup, sine_lookup)
    grad_projected_rows = jnp.concatenate([grad_query_rows.reshape(sequence_length, QUERY_HEADS * HEAD_SIZE), grad_key_rows.reshape(sequence_length, KEY_VALUE_HEADS * HEAD_SIZE), grad_value_rows.reshape(sequence_length, KEY_VALUE_HEADS * HEAD_SIZE)], axis=-1).astype(jnp.bfloat16)
    grad_qkv = inner_rows(hidden_attn, grad_projected_rows)
    d_hidden_attn = outer_column_count(grad_projected_rows, query_key_value_weight)
    grad_gain_attn = lax.optimization_barrier(jnp.sum(d_hidden_attn * normed_attn, axis=0))
    d_inputs = (d_mid + norm_back(d_hidden_attn, normed_attn, inv_attn, gain_one)).astype(jnp.bfloat16)
    flat_grads = jnp.concatenate([grad_qkv.reshape(-1), grad_out.reshape(-1), grad_gateup.reshape(-1), grad_down.reshape(-1), grad_gain_attn, grad_gain_ffn])
    return (outputs, d_inputs, flat_grads)

def adam_update(grads, clip_factor, params, moment_one, moment_two, decay_mask):
    clipped = grads * clip_factor
    new_moment_one = beta_one * moment_one + (1.0 - beta_one) * clipped
    new_moment_two = beta_two * moment_two + (1.0 - beta_two) * clipped * clipped
    step_size = new_moment_one / bias_one / (jnp.sqrt(new_moment_two / bias_two) + adam_eps)
    decay_term = jnp.where(decay_mask, decay_rate * params, jnp.zeros_like(params))
    new_params = params - learn_rate * (step_size + decay_term)
    return (new_params, new_moment_one, new_moment_two)

def reference(inputs, segments, cotangent, params, moment_one, moment_two):
    weights = unpack(params.astype(jnp.bfloat16))
    block_rows = math.gcd(ROWS, max(1, 4096 // LEN))
    blocks = ROWS // block_rows
    inputs_blocked = inputs.reshape(blocks, block_rows, LEN, MODEL_WIDTH)
    segments_blocked = segments.reshape(blocks, block_rows, LEN)
    cotangent_blocked = cotangent.reshape(blocks, block_rows, LEN, MODEL_WIDTH)

    def row_block(running, blocked):
        outs_rows, dins_rows, grads_rows = jax.vmap(layer_row, in_axes=(0, 0, 0, None))(blocked[0], blocked[1], blocked[2], weights)
        rounded = lax.optimization_barrier(grads_rows.astype(jnp.bfloat16))
        return (running + lax.optimization_barrier(jnp.sum(rounded.astype(jnp.float32), axis=0)), (outs_rows, dins_rows))
    grads, stacked = lax.scan(row_block, jnp.zeros((NPARAM,), jnp.float32), (inputs_blocked, segments_blocked, cotangent_blocked))
    outputs = stacked[0].reshape(ROWS, LEN, MODEL_WIDTH)
    d_inputs = stacked[1].reshape(ROWS, LEN, MODEL_WIDTH)
    squares = jnp.sum(grads * grads)
    clip_factor = jnp.minimum(jnp.float32(1.0), max_norm * lax.rsqrt(squares))
    decay_mask = jnp.arange(NPARAM, dtype=jnp.int32) < NPARAM - 2 * MODEL_WIDTH
    new_params, new_moment_one, new_moment_two = adam_update(grads, clip_factor, params, moment_one, moment_two, decay_mask)
    return (outputs, d_inputs, grads, new_params, new_moment_one, new_moment_two)
```

```python
import functools
import math

import jax
import jax.numpy as jnp
from jax import lax
from jax.experimental import pallas as pl
from jax.experimental.pallas import tpu as pltpu
from jax.sharding import PartitionSpec as P

MESH = pl.DeviceIdType.MESH
LANES = 128

MODEL_WIDTH = 576
QUERY_HEADS = 9
KEY_VALUE_HEADS = 3
HEAD_SIZE = 64
FF = 1536


norm_eps = 1e-05
theta_base = 10000.0
masked_value = -1e30
beta_one = 0.9
beta_two = 0.95
bias_one = 0.19
bias_two = 0.0975
learn_rate = 0.03
decay_rate = 0.1
adam_eps = 1e-08
max_norm = 1.0


def contract(pattern, left_op, right_op):
    return jnp.einsum(pattern, left_op, right_op, preferred_element_type=jnp.float32)


def inner_rows(left_op, right_op):
    return lax.dot_general(
        left_op, right_op, (((0,), (0,)), ((), ())), preferred_element_type=jnp.float32
    )


def outer_column_count(left_op, right_op):
    return lax.dot_general(
        left_op, right_op, (((1,), (1,)), ((), ())), preferred_element_type=jnp.float32
    )


def unpack(main, gains):
    query_key_value_width = (QUERY_HEADS + 2 * KEY_VALUE_HEADS) * HEAD_SIZE
    shapes = [
        (MODEL_WIDTH, query_key_value_width),
        (QUERY_HEADS * HEAD_SIZE, MODEL_WIDTH),
        (MODEL_WIDTH, 2 * FF),
        (FF, MODEL_WIDTH),
    ]
    pieces = []
    offset = 0
    for piece_shape in shapes:
        extent = math.prod(piece_shape) // LANES
        pieces.append(main[offset : offset + extent].reshape(piece_shape))
        offset += extent
    return pieces + [gains[:MODEL_WIDTH], gains[MODEL_WIDTH:]]


def positions_of(segment_row):
    index_row = jnp.arange(segment_row.shape[0], dtype=jnp.int32)
    previous = jnp.concatenate([segment_row[:1] - 1, segment_row[:-1]])
    starts = jnp.where(segment_row != previous, index_row, jnp.zeros_like(index_row))
    return index_row - lax.cummax(starts, axis=0)


def rope_tables(positions):
    half_size = HEAD_SIZE // 2
    freqs = theta_base ** (-2.0 * jnp.arange(half_size, dtype=jnp.float32) / HEAD_SIZE)
    angles = positions.astype(jnp.float32)[:, None] * freqs[None, :]
    return (jnp.cos(angles)[:, None, :], jnp.sin(angles)[:, None, :])


def apply_rotation(vectors, cosine_lookup, sine_lookup):
    half_size = HEAD_SIZE // 2
    first_half = vectors[..., :half_size]
    second_half = vectors[..., half_size:]
    return jnp.concatenate(
        [
            first_half * cosine_lookup - second_half * sine_lookup,
            second_half * cosine_lookup + first_half * sine_lookup,
        ],
        axis=-1,
    )


def unrotate(vectors, cosine_lookup, sine_lookup):
    half_size = HEAD_SIZE // 2
    first_half = vectors[..., :half_size]
    second_half = vectors[..., half_size:]
    return jnp.concatenate(
        [
            first_half * cosine_lookup + second_half * sine_lookup,
            second_half * cosine_lookup - first_half * sine_lookup,
        ],
        axis=-1,
    )


def norm_back(d_hidden, normed, inverse, gain):
    d_normed = d_hidden * gain
    return inverse * (d_normed - normed * jnp.mean(d_normed * normed, axis=-1, keepdims=True))


def layer_row(inputs, segment_row, cotangent, weights):
    query_key_value_weight, output_weight, w_gateup, w_down, gain_attn, gain_ffn = weights
    sequence_length = inputs.shape[0]
    repeat_count = QUERY_HEADS // KEY_VALUE_HEADS
    scale_factor = HEAD_SIZE ** (-0.5)
    gain_one = gain_attn.astype(jnp.float32)
    gain_two = gain_ffn.astype(jnp.float32)
    resid_in = inputs.astype(jnp.float32)
    inv_attn = lax.rsqrt(jnp.mean(resid_in * resid_in, axis=-1, keepdims=True) + norm_eps)
    normed_attn = resid_in * inv_attn
    hidden_attn = (normed_attn * gain_one).astype(jnp.bfloat16)
    projected_output = jnp.dot(
        hidden_attn, query_key_value_weight, preferred_element_type=jnp.float32
    )
    cosine_lookup, sine_lookup = rope_tables(positions_of(segment_row))
    query_rows = projected_output[:, : QUERY_HEADS * HEAD_SIZE].reshape(
        sequence_length, QUERY_HEADS, HEAD_SIZE
    )
    key_matrix = projected_output[
        :, QUERY_HEADS * HEAD_SIZE : (QUERY_HEADS + KEY_VALUE_HEADS) * HEAD_SIZE
    ].reshape(sequence_length, KEY_VALUE_HEADS, HEAD_SIZE)
    query_rows_rotated = (
        apply_rotation(query_rows, cosine_lookup, sine_lookup)
        .astype(jnp.bfloat16)
        .reshape(sequence_length, KEY_VALUE_HEADS, repeat_count, HEAD_SIZE)
    )
    keys_rot = apply_rotation(key_matrix, cosine_lookup, sine_lookup).astype(jnp.bfloat16)
    value_rows = (
        projected_output[:, (QUERY_HEADS + KEY_VALUE_HEADS) * HEAD_SIZE :]
        .reshape(sequence_length, KEY_VALUE_HEADS, HEAD_SIZE)
        .astype(jnp.bfloat16)
    )
    index_row = jnp.arange(sequence_length)
    allowed = (segment_row[:, None] == segment_row[None, :]) & (
        index_row[:, None] >= index_row[None, :]
    )
    scores = contract("qgrd,kgd->grqk", query_rows_rotated, keys_rot) * scale_factor
    scores = jnp.where(allowed, scores, masked_value)
    peak = jnp.max(scores, axis=-1, keepdims=True)
    log_total = peak + jnp.log(jnp.sum(jnp.exp(scores - peak), axis=-1, keepdims=True))
    probs_b = jnp.exp(scores - log_total).astype(jnp.bfloat16)
    attended = (
        contract("grqk,kgd->qgrd", probs_b, value_rows)
        .astype(jnp.bfloat16)
        .reshape(sequence_length, QUERY_HEADS * HEAD_SIZE)
    )
    mid = resid_in + jnp.dot(attended, output_weight, preferred_element_type=jnp.float32)
    inv_ffn = lax.rsqrt(jnp.mean(mid * mid, axis=-1, keepdims=True) + norm_eps)
    normed_ffn = mid * inv_ffn
    hidden_ffn = (normed_ffn * gain_two).astype(jnp.bfloat16)
    gate_up = jnp.dot(hidden_ffn, w_gateup, preferred_element_type=jnp.float32)
    gate_pre = gate_up[:, :FF]
    upper = gate_up[:, FF:]
    sigmoid_gate = jax.nn.sigmoid(gate_pre)
    activation = (gate_pre * sigmoid_gate * upper).astype(jnp.bfloat16)
    outputs = (mid + jnp.dot(activation, w_down, preferred_element_type=jnp.float32)).astype(
        jnp.bfloat16
    )
    grad_down = inner_rows(activation, cotangent)
    d_act = outer_column_count(cotangent, w_down)
    d_gate = d_act * upper * sigmoid_gate * (1.0 + gate_pre * (1.0 - sigmoid_gate))
    d_upper = d_act * gate_pre * sigmoid_gate
    d_gate_up = jnp.concatenate([d_gate, d_upper], axis=-1).astype(jnp.bfloat16)
    grad_gateup = inner_rows(hidden_ffn, d_gate_up)
    d_hidden_ffn = outer_column_count(d_gate_up, w_gateup)
    grad_gain_ffn = jnp.sum(d_hidden_ffn * normed_ffn, axis=0)
    d_mid = cotangent.astype(jnp.float32) + norm_back(d_hidden_ffn, normed_ffn, inv_ffn, gain_two)
    grad_middle_batch = d_mid.astype(jnp.bfloat16)
    grad_out = inner_rows(attended, grad_middle_batch)
    grad_attended_rows = (
        outer_column_count(grad_middle_batch, output_weight)
        .astype(jnp.bfloat16)
        .reshape(sequence_length, KEY_VALUE_HEADS, repeat_count, HEAD_SIZE)
    )
    recomputed = contract("qgrd,kgd->grqk", query_rows_rotated, keys_rot) * scale_factor
    probs = jnp.exp(jnp.where(allowed, recomputed, masked_value) - log_total)
    d_probs = contract("qgrd,kgd->grqk", grad_attended_rows, value_rows)
    row_total = jnp.sum(probs * d_probs, axis=-1, keepdims=True)
    d_scores = (probs * (d_probs - row_total) * scale_factor).astype(jnp.bfloat16)
    grad_query_rows = contract("grqk,kgd->qgrd", d_scores, keys_rot).reshape(
        sequence_length, QUERY_HEADS, HEAD_SIZE
    )
    grad_key_rows = contract("grqk,qgrd->kgd", d_scores, query_rows_rotated)
    grad_value_rows = contract("grqk,qgrd->kgd", probs_b, grad_attended_rows)
    grad_query_rows = unrotate(grad_query_rows, cosine_lookup, sine_lookup)
    grad_key_rows = unrotate(grad_key_rows, cosine_lookup, sine_lookup)
    grad_projected_rows = jnp.concatenate(
        [
            grad_query_rows.reshape(sequence_length, QUERY_HEADS * HEAD_SIZE),
            grad_key_rows.reshape(sequence_length, KEY_VALUE_HEADS * HEAD_SIZE),
            grad_value_rows.reshape(sequence_length, KEY_VALUE_HEADS * HEAD_SIZE),
        ],
        axis=-1,
    ).astype(jnp.bfloat16)
    grad_qkv = inner_rows(hidden_attn, grad_projected_rows)
    d_hidden_attn = outer_column_count(grad_projected_rows, query_key_value_weight)
    grad_gain_attn = jnp.sum(d_hidden_attn * normed_attn, axis=0)
    d_inputs = (d_mid + norm_back(d_hidden_attn, normed_attn, inv_attn, gain_one)).astype(
        jnp.bfloat16
    )
    matrices = [grad_qkv, grad_out, grad_gateup, grad_down]
    main = jnp.concatenate([m.astype(jnp.bfloat16).reshape(-1, LANES) for m in matrices])
    gains = jnp.concatenate([grad_gain_attn, grad_gain_ffn])
    return (outputs, d_inputs, main, gains)


def adam_update(grads, clip_factor, params, moment_one, moment_two, decay_mask):
    clipped = grads * clip_factor
    new_moment_one = beta_one * moment_one + (1.0 - beta_one) * clipped
    new_moment_two = beta_two * moment_two + (1.0 - beta_two) * clipped * clipped
    step_size = new_moment_one / bias_one / (jnp.sqrt(new_moment_two / bias_two) + adam_eps)
    decay_term = jnp.where(decay_mask, decay_rate * params, jnp.zeros_like(params))
    new_params = params - learn_rate * (step_size + decay_term)
    return (new_params, new_moment_one, new_moment_two)


def my_bits(wide, count):
    return [(wide // 2**b) % 2 for b in range(count)]


def flipped(wide, bit, b):
    return wide + (1 - 2 * bit) * 2**b


def greet(wide, group, bits, groups):
    barrier = pltpu.get_barrier_semaphore()
    peers = [(flipped(wide, bit, b), group) for b, bit in enumerate(bits)]
    peers += [(wide, (group + d) % groups) for d in range(1, groups)]
    for peer in peers:
        pl.semaphore_signal(barrier, inc=1, device_id=peer, device_id_type=MESH)
    pl.semaphore_wait(barrier, len(peers))


def send(src, dst, send_sem, recv_sem, peer):
    copy = pltpu.make_async_remote_copy(
        src_ref=src,
        dst_ref=dst,
        send_sem=send_sem,
        recv_sem=recv_sem,
        device_id=peer,
        device_id_type=MESH,
    )
    copy.start()
    return copy


def bit_order(chunk, count):
    rest = list(range(1, count))
    return [0] + (rest if chunk % 2 == 0 else rest[::-1])


def tails_kernel(groups, bits_count, tail_ref, out_ref, send_sem, recv_sem):
    wide, group = lax.axis_index("wide"), lax.axis_index("group")
    greet(wide, group, [], groups)
    out_ref[pl.ds(group, 1)] = tail_ref[...][None]
    copies = []
    for d in range(1, groups):
        copies.append(
            send(
                tail_ref,
                out_ref.at[group],
                send_sem.at[d - 1],
                recv_sem.at[d - 1],
                (wide, (group + d) % groups),
            )
        )
    for copy in copies:
        copy.wait()


def gather_kernel(groups, count, chunks, block_ref, out_ref, own_sem, zs, zr, ws, wr):
    wide, group = lax.axis_index("wide"), lax.axis_index("group")
    bits = my_bits(wide, count)
    step = block_ref.shape[-2] // chunks
    greet(wide, group, bits, groups)

    def place(ref, lead, open_bits, chunk):
        index = [slice(None) if b in open_bits else bits[b] for b in reversed(range(count))]
        return ref.at[tuple(lead + index + [pl.ds(chunk * step, step)])]

    units = [(d, c) for d in range(1, groups) for c in range(chunks)]
    copies = {}
    for u, (d, c) in enumerate(units):
        copies[u, 0] = send(
            place(block_ref, [], [], c),
            place(out_ref, [group], [], c),
            zs.at[u],
            zr.at[u],
            (wide, (group + d) % groups),
        )
    own = pltpu.make_async_copy(block_ref, out_ref.at[group], own_sem)
    own.start()
    for tick in range(len(units) // chunks + count + 1):
        for u, (d, c) in enumerate(units):
            stage = tick - u // chunks
            if not 0 <= stage <= count:
                continue
            copies[u, stage].wait_recv()
            if stage == count:
                continue
            order = bit_order(c, count)[::-1]
            b = order[stage]
            source = (group + groups - d) % groups
            here = place(out_ref, [source], order[:stage], c)
            copies[u, stage + 1] = send(
                here, here, ws.at[u, stage], wr.at[u, stage], (flipped(wide, bits[b], b), group)
            )
    for copy in copies.values():
        copy.wait_send()
    own.wait()


def sum_kernel(groups, count, chunks, x_ref, gain_ref, out_ref, head_ref, gsum_ref, sq_ref, *scratch):
    recvs, accs = scratch[:count], scratch[count : 2 * count]
    recv_z, gain_w, gain_z, sq_z, piece_head = scratch[2 * count : 2 * count + 5]
    ss, sr, zs, zr, gs, gr, xs, xr, gzs, gzr, qs, qr, hs, hr = scratch[2 * count + 5 :]
    wide, group = lax.axis_index("wide"), lax.axis_index("group")
    bits = my_bits(wide, count)
    step = x_ref.shape[-2] // chunks
    greet(wide, group, bits, groups)
    copies = {}
    f32 = jnp.float32

    def partner(b):
        return (flipped(wide, bits[b], b), group)

    def part(c, stage, value):
        order = bit_order(c, count)
        left = sorted(order[stage:], reverse=True)
        return [value if b == order[stage] else slice(None) for b in left]

    def held(c, stage):
        return x_ref if stage == 0 else accs[stage - 1].at[c]

    def view(c, stage, flip):
        b = bit_order(c, count)[stage]
        index = [slice(None)] + part(c, stage, 1 - bits[b] if flip else bits[b])
        if stage == 0:
            index += [slice(None)] * (count + 2 - len(index) - 1)
            return x_ref.at[tuple(index + [pl.ds(c * step, step)])]
        return accs[stage - 1].at[tuple([c] + index)]

    def start_scatter(c, stage):
        b = bit_order(c, count)[stage]
        copies["s", c, stage] = send(
            view(c, stage, True), recvs[stage].at[c], ss.at[c, stage], sr.at[c, stage], partner(b)
        )

    def add_scatter(c, stage):
        copies["s", c, stage].wait_recv()
        mine, other, total = view(c, stage, False), recvs[stage].at[c], accs[stage].at[c]

        def body(i, _):
            total[i] = (mine[i].astype(f32) + other[i].astype(f32)).astype(jnp.bfloat16)
            return 0

        lax.fori_loop(0, groups, body, 0)

    def start_groups(c):
        for d in range(1, groups):
            to = (group + d) % groups
            copies["z", c, d] = send(
                accs[-1].at[c, to],
                recv_z.at[c, d - 1],
                zs.at[c, d - 1],
                zr.at[c, d - 1],
                (wide, to),
            )

    def place(open_bits, c):
        index = [slice(None) if b in open_bits else bits[b] for b in reversed(range(count))]
        return out_ref.at[tuple(index + [pl.ds(c * step, step)])]

    def add_groups(c):
        total = accs[-1][c, group].astype(f32)
        for d in range(1, groups):
            copies["z", c, d].wait_recv()
            total = total + recv_z[c, d - 1].astype(f32)
        place([], c)[...] = total.astype(jnp.bfloat16)

    def start_gather(c, stage):
        order = bit_order(c, count)[::-1]
        here = place(order[:stage], c)
        copies["g", c, stage] = send(
            here, here, gs.at[c, stage], gr.at[c, stage], partner(order[stage])
        )

    for c in range(chunks):
        start_scatter(c, 0)
    gain_w[0] = gain_ref[...]
    copies["x", 0] = send(gain_w.at[0], gain_w.at[count + 1], xs.at[0], xr.at[0], partner(0))

    for tick in range(chunks // 2 + 2 * count + 1):
        for c in range(chunks):
            s = tick - c // 2
            if 0 <= s < count:
                add_scatter(c, s)
                if s + 1 < count:
                    start_scatter(c, s + 1)
                else:
                    start_groups(c)
            elif s == count:
                add_groups(c)
                start_gather(c, 0)
            elif count < s <= 2 * count:
                copies["g", c, s - count - 1].wait_recv()
                if s < 2 * count:
                    start_gather(c, s - count)
        if tick < count:
            copies["x", tick].wait_recv()
            gain_w[tick + 1] = gain_w[tick] + gain_w[count + 1 + tick]
            if tick + 1 < count:
                copies["x", tick + 1] = send(
                    gain_w.at[tick + 1],
                    gain_w.at[count + 2 + tick],
                    xs.at[tick + 1],
                    xr.at[tick + 1],
                    partner(tick + 1),
                )
            else:
                gain_z[pl.ds(group, 1)] = gain_w[pl.ds(count, 1)]
                for d in range(1, groups):
                    copies["gz", d] = send(
                        gain_w.at[count],
                        gain_z.at[group],
                        gzs.at[d - 1],
                        gzr.at[d - 1],
                        (wide, (group + d) % groups),
                    )

    first = tuple([0] * count + [pl.ds(0, 16)])
    copies["h"] = send(out_ref.at[first], head_ref, hs, hr, (wide, (group + groups - 1) % groups))
    flat_lead = out_ref.shape[:-2]

    def squares(i, total):
        index = tuple((i // 2**b) % 2 for b in reversed(range(len(flat_lead))))
        value = out_ref[index].astype(f32)
        value = value * value
        return total + jnp.sum(value.reshape(-1, 8, LANES), axis=0)

    square = lax.fori_loop(0, math.prod(flat_lead), squares, jnp.zeros((8, LANES), f32))
    piece_head[...] = square
    sq_z[pl.ds(group, 1)] = square[None]
    for d in range(1, groups):
        copies["q", d] = send(
            piece_head, sq_z.at[group], qs.at[d - 1], qr.at[d - 1], (wide, (group + d) % groups)
        )
    for d in range(1, groups):
        copies["gz", d].wait_recv()
    gains = gain_z[0]
    for d in range(1, groups):
        gains = gains + gain_z[d]
    gsum_ref[...] = gains
    for d in range(1, groups):
        copies["q", d].wait_recv()
    square = sq_z[0]
    for d in range(1, groups):
        square = square + sq_z[d]
    sq_ref[...] = square
    copies["h"].wait_recv()
    for copy in copies.values():
        copy.wait_send()


def params_of(identity):
    return pltpu.CompilerParams(
        collective_id=identity, has_side_effects=True, vmem_limit_bytes=60 * 2**20
    )


def vmem_specs(n):
    return [pl.BlockSpec(memory_space=pltpu.VMEM)] * n


def gather_tails(tail, groups):
    dma = pltpu.SemaphoreType.DMA
    return pl.pallas_call(
        functools.partial(tails_kernel, groups, 0),
        out_shape=jax.ShapeDtypeStruct((groups,) + tail.shape, tail.dtype),
        in_specs=vmem_specs(1),
        out_specs=vmem_specs(1)[0],
        scratch_shapes=[dma((groups - 1,)), dma((groups - 1,))],
        compiler_params=params_of(0),
        name="tails",
    )(tail)


def gather_blocks(block, groups, count, chunks):
    dma = pltpu.SemaphoreType.DMA
    units = (groups - 1) * chunks
    return pl.pallas_call(
        functools.partial(gather_kernel, groups, count, chunks),
        out_shape=jax.ShapeDtypeStruct((groups,) + block.shape, block.dtype),
        in_specs=vmem_specs(1),
        out_specs=vmem_specs(1)[0],
        scratch_shapes=[
            dma,
            dma((units,)),
            dma((units,)),
            dma((units, count)),
            dma((units, count)),
        ],
        compiler_params=params_of(1),
        name="gather_weights",
    )(block)


def sum_blocks(main, gains, groups, count, chunks):
    dma = pltpu.SemaphoreType.DMA
    rows = main.shape[-2]
    step = rows // chunks
    bf16, f32 = jnp.bfloat16, jnp.float32
    stages = [
        pltpu.VMEM((chunks, groups) + (2,) * (count - 1 - k) + (step, LANES), bf16)
        for k in range(count)
    ]
    return pl.pallas_call(
        functools.partial(sum_kernel, groups, count, chunks),
        out_shape=(
            jax.ShapeDtypeStruct((2,) * count + (rows, LANES), bf16),
            jax.ShapeDtypeStruct((16, LANES), bf16),
            jax.ShapeDtypeStruct(gains.shape, f32),
            jax.ShapeDtypeStruct((8, LANES), f32),
        ),
        in_specs=vmem_specs(2),
        out_specs=tuple(vmem_specs(4)),
        scratch_shapes=stages
        + stages
        + [
            pltpu.VMEM((chunks, groups - 1, step, LANES), bf16),
            pltpu.VMEM((2 * count + 1,) + gains.shape, f32),
            pltpu.VMEM((groups,) + gains.shape, f32),
            pltpu.VMEM((groups, 8, LANES), f32),
            pltpu.VMEM((8, LANES), f32),
        ]
        + [dma((chunks, count))] * 2
        + [dma((chunks, groups - 1))] * 2
        + [dma((chunks, count))] * 2
        + [dma((count,))] * 2
        + [dma((groups - 1,))] * 4
        + [dma, dma],
        compiler_params=params_of(2),
        name="sum_grads",
    )(main, gains)


def on_device(inputs, segments, cotangent, params, moment_one, moment_two):
    groups = lax.axis_size("group")
    wides = lax.axis_size("wide")
    group = lax.axis_index("group")
    count = wides.bit_length() - 1
    share_len = params.shape[0]
    gain_len = 2 * MODEL_WIDTH
    extra = gain_len // groups
    block_len = share_len - extra
    block_rows = block_len // LANES
    piece_rows = -(-block_rows // wides)
    chunks = 6 if piece_rows % 96 == 0 else 2
    piece_rows = -(-piece_rows // (16 * chunks)) * 16 * chunks
    padding = piece_rows * wides - block_rows
    lead = (2,) * count

    def to_pieces(rows):
        rows = rows.reshape(-1, block_rows, LANES)
        if padding:
            rows = jnp.pad(rows, ((0, 0), (0, padding), (0, 0)))
        return rows.reshape((-1,) + lead + (piece_rows, LANES))

    def from_pieces(pieces):
        rows = pieces.reshape(-1, piece_rows * wides, LANES)[:, :block_rows]
        return rows.reshape(-1, LANES)

    rounded = params.astype(jnp.bfloat16)
    tail = jnp.pad(rounded[share_len - gain_len :], (0, 16 * LANES - gain_len)).reshape(16, LANES)
    tails = gather_tails(tail, groups).reshape(groups, -1)[:, :gain_len]
    before = lax.dynamic_index_in_dim(tails, (group + groups - 1) % groups, keepdims=False)
    joined = jnp.concatenate([before, rounded])
    block = lax.dynamic_slice(joined, (gain_len - extra * group,), (block_len,))
    gathered = gather_blocks(to_pieces(block)[0], groups, count, 2)
    weights = unpack(from_pieces(gathered), tails[groups - 1])
    outputs, d_inputs, main, gains = layer_row(inputs[0], segments[0], cotangent[0], weights)
    gains = gains.astype(jnp.bfloat16).astype(jnp.float32)
    gains = jnp.pad(gains, (0, 16 * LANES - gain_len)).reshape(16, LANES)
    summed_block, head, gains, square = sum_blocks(to_pieces(main), gains, groups, count, chunks)
    gains = gains.reshape(-1)[:gain_len].astype(jnp.bfloat16)
    head = jnp.where(group == groups - 1, gains, head.reshape(-1)[:gain_len])
    joined = jnp.concatenate([from_pieces(summed_block).reshape(-1), head])
    summed = lax.dynamic_slice(joined, (extra * group,), (share_len,)).astype(jnp.float32)
    gains = gains.astype(jnp.float32)
    squares = jnp.sum(square) + jnp.sum(gains * gains)
    clip_factor = jnp.minimum(jnp.float32(1.0), max_norm * lax.rsqrt(squares))
    flat_index = group * share_len + jnp.arange(share_len, dtype=jnp.int32)
    decay_mask = flat_index < share_len * groups - gain_len
    new_params, new_moment_one, new_moment_two = adam_update(
        summed, clip_factor, params, moment_one, moment_two, decay_mask
    )
    return (outputs[None], d_inputs[None], summed, new_params, new_moment_one, new_moment_two)


def solution(mesh):
    return jax.shard_map(
        on_device,
        mesh=mesh,
        in_specs=(
            P(("wide", "group"), None, None),
            P(("wide", "group"), None),
            P(("wide", "group"), None, None),
            P("group"),
            P("group"),
            P("group"),
        ),
        out_specs=(
            P(("wide", "group"), None, None),
            P(("wide", "group"), None, None),
            P("group"),
            P("group"),
            P("group"),
            P("group"),
        ),
        check_vma=False,
    )
```

```python
import functools
import math

import jax
import jax.numpy as jnp
from jax import lax
from jax.experimental import pallas as pl
from jax.experimental.pallas import tpu as pltpu
from jax.sharding import PartitionSpec as P

MESH = pl.DeviceIdType.MESH
LANES = 128

MODEL_WIDTH = 576
QUERY_HEADS = 9
KEY_VALUE_HEADS = 3
HEAD_SIZE = 64
FF = 1536


norm_eps = 1e-05
theta_base = 10000.0
masked_value = -1e30
beta_one = 0.9
beta_two = 0.95
bias_one = 0.19
bias_two = 0.0975
learn_rate = 0.03
decay_rate = 0.1
adam_eps = 1e-08
max_norm = 1.0


def contract(pattern, left_op, right_op):
    return jnp.einsum(pattern, left_op, right_op, preferred_element_type=jnp.float32)


def inner_rows(left_op, right_op):
    return lax.dot_general(
        left_op, right_op, (((0,), (0,)), ((), ())), preferred_element_type=jnp.float32
    )


def outer_column_count(left_op, right_op):
    return lax.dot_general(
        left_op, right_op, (((1,), (1,)), ((), ())), preferred_element_type=jnp.float32
    )


def unpack(main, gains):
    query_key_value_width = (QUERY_HEADS + 2 * KEY_VALUE_HEADS) * HEAD_SIZE
    shapes = [
        (MODEL_WIDTH, query_key_value_width),
        (QUERY_HEADS * HEAD_SIZE, MODEL_WIDTH),
        (MODEL_WIDTH, 2 * FF),
        (FF, MODEL_WIDTH),
    ]
    pieces = []
    offset = 0
    for piece_shape in shapes:
        extent = math.prod(piece_shape) // LANES
        pieces.append(main[offset : offset + extent].reshape(piece_shape))
        offset += extent
    return pieces + [gains[:MODEL_WIDTH], gains[MODEL_WIDTH:]]


def positions_of(segment_row):
    index_row = jnp.arange(segment_row.shape[0], dtype=jnp.int32)
    previous = jnp.concatenate([segment_row[:1] - 1, segment_row[:-1]])
    starts = jnp.where(segment_row != previous, index_row, jnp.zeros_like(index_row))
    return index_row - lax.cummax(starts, axis=0)


def rope_tables(positions):
    half_size = HEAD_SIZE // 2
    freqs = theta_base ** (-2.0 * jnp.arange(half_size, dtype=jnp.float32) / HEAD_SIZE)
    angles = positions.astype(jnp.float32)[:, None] * freqs[None, :]
    return (jnp.cos(angles)[:, None, :], jnp.sin(angles)[:, None, :])


def apply_rotation(vectors, cosine_lookup, sine_lookup):
    half_size = HEAD_SIZE // 2
    first_half = vectors[..., :half_size]
    second_half = vectors[..., half_size:]
    return jnp.concatenate(
        [
            first_half * cosine_lookup - second_half * sine_lookup,
            second_half * cosine_lookup + first_half * sine_lookup,
        ],
        axis=-1,
    )


def unrotate(vectors, cosine_lookup, sine_lookup):
    half_size = HEAD_SIZE // 2
    first_half = vectors[..., :half_size]
    second_half = vectors[..., half_size:]
    return jnp.concatenate(
        [
            first_half * cosine_lookup + second_half * sine_lookup,
            second_half * cosine_lookup - first_half * sine_lookup,
        ],
        axis=-1,
    )


def norm_back(d_hidden, normed, inverse, gain):
    d_normed = d_hidden * gain
    return inverse * (d_normed - normed * jnp.mean(d_normed * normed, axis=-1, keepdims=True))


def layer_row(inputs, segment_row, cotangent, weights):
    query_key_value_weight, output_weight, w_gateup, w_down, gain_attn, gain_ffn = weights
    sequence_length = inputs.shape[0]
    repeat_count = QUERY_HEADS // KEY_VALUE_HEADS
    scale_factor = HEAD_SIZE ** (-0.5)
    gain_one = gain_attn.astype(jnp.float32)
    gain_two = gain_ffn.astype(jnp.float32)
    resid_in = inputs.astype(jnp.float32)
    inv_attn = lax.rsqrt(jnp.mean(resid_in * resid_in, axis=-1, keepdims=True) + norm_eps)
    normed_attn = resid_in * inv_attn
    hidden_attn = (normed_attn * gain_one).astype(jnp.bfloat16)
    projected_output = jnp.dot(
        hidden_attn, query_key_value_weight, preferred_element_type=jnp.float32
    )
    cosine_lookup, sine_lookup = rope_tables(positions_of(segment_row))
    query_rows = projected_output[:, : QUERY_HEADS * HEAD_SIZE].reshape(
        sequence_length, QUERY_HEADS, HEAD_SIZE
    )
    key_matrix = projected_output[
        :, QUERY_HEADS * HEAD_SIZE : (QUERY_HEADS + KEY_VALUE_HEADS) * HEAD_SIZE
    ].reshape(sequence_length, KEY_VALUE_HEADS, HEAD_SIZE)
    query_rows_rotated = (
        apply_rotation(query_rows, cosine_lookup, sine_lookup)
        .astype(jnp.bfloat16)
        .reshape(sequence_length, KEY_VALUE_HEADS, repeat_count, HEAD_SIZE)
    )
    keys_rot = apply_rotation(key_matrix, cosine_lookup, sine_lookup).astype(jnp.bfloat16)
    value_rows = (
        projected_output[:, (QUERY_HEADS + KEY_VALUE_HEADS) * HEAD_SIZE :]
        .reshape(sequence_length, KEY_VALUE_HEADS, HEAD_SIZE)
        .astype(jnp.bfloat16)
    )
    index_row = jnp.arange(sequence_length)
    allowed = (segment_row[:, None] == segment_row[None, :]) & (
        index_row[:, None] >= index_row[None, :]
    )
    scores = contract("qgrd,kgd->grqk", query_rows_rotated, keys_rot) * scale_factor
    scores = jnp.where(allowed, scores, masked_value)
    peak = jnp.max(scores, axis=-1, keepdims=True)
    log_total = peak + jnp.log(jnp.sum(jnp.exp(scores - peak), axis=-1, keepdims=True))
    probs_b = jnp.exp(scores - log_total).astype(jnp.bfloat16)
    attended = (
        contract("grqk,kgd->qgrd", probs_b, value_rows)
        .astype(jnp.bfloat16)
        .reshape(sequence_length, QUERY_HEADS * HEAD_SIZE)
    )
    mid = resid_in + jnp.dot(attended, output_weight, preferred_element_type=jnp.float32)
    inv_ffn = lax.rsqrt(jnp.mean(mid * mid, axis=-1, keepdims=True) + norm_eps)
    normed_ffn = mid * inv_ffn
    hidden_ffn = (normed_ffn * gain_two).astype(jnp.bfloat16)
    gate_up = jnp.dot(hidden_ffn, w_gateup, preferred_element_type=jnp.float32)
    gate_pre = gate_up[:, :FF]
    upper = gate_up[:, FF:]
    sigmoid_gate = jax.nn.sigmoid(gate_pre)
    activation = (gate_pre * sigmoid_gate * upper).astype(jnp.bfloat16)
    outputs = (mid + jnp.dot(activation, w_down, preferred_element_type=jnp.float32)).astype(
        jnp.bfloat16
    )
    grad_down = inner_rows(activation, cotangent)
    d_act = outer_column_count(cotangent, w_down)
    d_gate = d_act * upper * sigmoid_gate * (1.0 + gate_pre * (1.0 - sigmoid_gate))
    d_upper = d_act * gate_pre * sigmoid_gate
    d_gate_up = jnp.concatenate([d_gate, d_upper], axis=-1).astype(jnp.bfloat16)
    grad_gateup = inner_rows(hidden_ffn, d_gate_up)
    d_hidden_ffn = outer_column_count(d_gate_up, w_gateup)
    grad_gain_ffn = jnp.sum(d_hidden_ffn * normed_ffn, axis=0)
    d_mid = cotangent.astype(jnp.float32) + norm_back(d_hidden_ffn, normed_ffn, inv_ffn, gain_two)
    grad_middle_batch = d_mid.astype(jnp.bfloat16)
    grad_out = inner_rows(attended, grad_middle_batch)
    grad_attended_rows = (
        outer_column_count(grad_middle_batch, output_weight)
        .astype(jnp.bfloat16)
        .reshape(sequence_length, KEY_VALUE_HEADS, repeat_count, HEAD_SIZE)
    )
    recomputed = contract("qgrd,kgd->grqk", query_rows_rotated, keys_rot) * scale_factor
    probs = jnp.exp(jnp.where(allowed, recomputed, masked_value) - log_total)
    d_probs = contract("qgrd,kgd->grqk", grad_attended_rows, value_rows)
    row_total = jnp.sum(probs * d_probs, axis=-1, keepdims=True)
    d_scores = (probs * (d_probs - row_total) * scale_factor).astype(jnp.bfloat16)
    grad_query_rows = contract("grqk,kgd->qgrd", d_scores, keys_rot).reshape(
        sequence_length, QUERY_HEADS, HEAD_SIZE
    )
    grad_key_rows = contract("grqk,qgrd->kgd", d_scores, query_rows_rotated)
    grad_value_rows = contract("grqk,qgrd->kgd", probs_b, grad_attended_rows)
    grad_query_rows = unrotate(grad_query_rows, cosine_lookup, sine_lookup)
    grad_key_rows = unrotate(grad_key_rows, cosine_lookup, sine_lookup)
    grad_projected_rows = jnp.concatenate(
        [
            grad_query_rows.reshape(sequence_length, QUERY_HEADS * HEAD_SIZE),
            grad_key_rows.reshape(sequence_length, KEY_VALUE_HEADS * HEAD_SIZE),
            grad_value_rows.reshape(sequence_length, KEY_VALUE_HEADS * HEAD_SIZE),
        ],
        axis=-1,
    ).astype(jnp.bfloat16)
    grad_qkv = inner_rows(hidden_attn, grad_projected_rows)
    d_hidden_attn = outer_column_count(grad_projected_rows, query_key_value_weight)
    grad_gain_attn = jnp.sum(d_hidden_attn * normed_attn, axis=0)
    d_inputs = (d_mid + norm_back(d_hidden_attn, normed_attn, inv_attn, gain_one)).astype(
        jnp.bfloat16
    )
    matrices = [grad_qkv, grad_out, grad_gateup, grad_down]
    main = jnp.concatenate([m.astype(jnp.bfloat16).reshape(-1, LANES) for m in matrices])
    gains = jnp.concatenate([grad_gain_attn, grad_gain_ffn])
    return (outputs, d_inputs, main, gains)


def adam_update(grads, clip_factor, params, moment_one, moment_two, decay_mask):
    clipped = grads * clip_factor
    new_moment_one = beta_one * moment_one + (1.0 - beta_one) * clipped
    new_moment_two = beta_two * moment_two + (1.0 - beta_two) * clipped * clipped
    step_size = new_moment_one / bias_one / (jnp.sqrt(new_moment_two / bias_two) + adam_eps)
    decay_term = jnp.where(decay_mask, decay_rate * params, jnp.zeros_like(params))
    new_params = params - learn_rate * (step_size + decay_term)
    return (new_params, new_moment_one, new_moment_two)


def my_bits(wide, count):
    return [(wide // 2**b) % 2 for b in range(count)]


def flipped(wide, bit, b):
    return wide + (1 - 2 * bit) * 2**b


def greet(wide, group, bits, groups):
    barrier = pltpu.get_barrier_semaphore()
    peers = [(flipped(wide, bit, b), group) for b, bit in enumerate(bits)]
    peers += [(wide, (group + d) % groups) for d in range(1, groups)]
    for peer in peers:
        pl.semaphore_signal(barrier, inc=1, device_id=peer, device_id_type=MESH)
    pl.semaphore_wait(barrier, len(peers))


def send(src, dst, send_sem, recv_sem, peer):
    copy = pltpu.make_async_remote_copy(
        src_ref=src,
        dst_ref=dst,
        send_sem=send_sem,
        recv_sem=recv_sem,
        device_id=peer,
        device_id_type=MESH,
    )
    copy.start()
    return copy


def bit_order(chunk, count):
    rest = list(range(1, count))
    return [0] + (rest if chunk % 2 == 0 else rest[::-1])


def tails_kernel(groups, bits_count, tail_ref, out_ref, send_sem, recv_sem):
    wide, group = lax.axis_index("wide"), lax.axis_index("group")
    greet(wide, group, [], groups)
    out_ref[pl.ds(group, 1)] = tail_ref[...][None]
    copies = []
    for d in range(1, groups):
        copies.append(
            send(
                tail_ref,
                out_ref.at[group],
                send_sem.at[d - 1],
                recv_sem.at[d - 1],
                (wide, (group + d) % groups),
            )
        )
    for copy in copies:
        copy.wait()


def gather_kernel(groups, count, chunks, block_ref, out_ref, own_sem, zs, zr, ws, wr):
    wide, group = lax.axis_index("wide"), lax.axis_index("group")
    bits = my_bits(wide, count)
    step = block_ref.shape[-2] // chunks
    greet(wide, group, bits, groups)

    def place(ref, lead, open_bits, chunk):
        index = [slice(None) if b in open_bits else bits[b] for b in reversed(range(count))]
        return ref.at[tuple(lead + index + [pl.ds(chunk * step, step)])]

    units = [(d, c) for d in range(1, groups) for c in range(chunks)]
    copies = {}
    for u, (d, c) in enumerate(units):
        copies[u, 0] = send(
            place(block_ref, [], [], c),
            place(out_ref, [group], [], c),
            zs.at[u],
            zr.at[u],
            (wide, (group + d) % groups),
        )
    own = pltpu.make_async_copy(block_ref, out_ref.at[group], own_sem)
    own.start()
    for tick in range(len(units) // chunks + count + 1):
        for u, (d, c) in enumerate(units):
            stage = tick - u // chunks
            if not 0 <= stage <= count:
                continue
            copies[u, stage].wait_recv()
            if stage == count:
                continue
            order = bit_order(c, count)[::-1]
            b = order[stage]
            source = (group + groups - d) % groups
            here = place(out_ref, [source], order[:stage], c)
            copies[u, stage + 1] = send(
                here, here, ws.at[u, stage], wr.at[u, stage], (flipped(wide, bits[b], b), group)
            )
    for copy in copies.values():
        copy.wait_send()
    own.wait()


def sum_kernel(groups, count, chunks, x_ref, gain_ref, out_ref, head_ref, gsum_ref, sq_ref, *scratch):
    recvs, accs = scratch[:count], scratch[count : 2 * count]
    recv_z, gain_w, gain_z, sq_z, piece_head = scratch[2 * count : 2 * count + 5]
    ss, sr, zs, zr, gs, gr, xs, xr, gzs, gzr, qs, qr, hs, hr = scratch[2 * count + 5 :]
    wide, group = lax.axis_index("wide"), lax.axis_index("group")
    bits = my_bits(wide, count)
    step = x_ref.shape[-2] // chunks
    greet(wide, group, bits, groups)
    copies = {}
    f32 = jnp.float32

    def partner(b):
        return (flipped(wide, bits[b], b), group)

    def part(c, stage, value):
        order = bit_order(c, count)
        left = sorted(order[stage:], reverse=True)
        return [value if b == order[stage] else slice(None) for b in left]

    def held(c, stage):
        return x_ref if stage == 0 else accs[stage - 1].at[c]

    def view(c, stage, flip):
        b = bit_order(c, count)[stage]
        index = [slice(None)] + part(c, stage, 1 - bits[b] if flip else bits[b])
        if stage == 0:
            index += [slice(None)] * (count + 2 - len(index) - 1)
            return x_ref.at[tuple(index + [pl.ds(c * step, step)])]
        return accs[stage - 1].at[tuple([c] + index)]

    def start_scatter(c, stage):
        b = bit_order(c, count)[stage]
        copies["s", c, stage] = send(
            view(c, stage, True), recvs[stage].at[c], ss.at[c, stage], sr.at[c, stage], partner(b)
        )

    def add_scatter(c, stage):
        copies["s", c, stage].wait_recv()
        mine, other, total = view(c, stage, False), recvs[stage].at[c], accs[stage].at[c]

        def body(i, _):
            total[i] = (mine[i].astype(f32) + other[i].astype(f32)).astype(jnp.bfloat16)
            return 0

        lax.fori_loop(0, groups, body, 0)

    def start_groups(c):
        for d in range(1, groups):
            to = (group + d) % groups
            copies["z", c, d] = send(
                accs[-1].at[c, to],
                recv_z.at[c, d - 1],
                zs.at[c, d - 1],
                zr.at[c, d - 1],
                (wide, to),
            )

    def place(open_bits, c):
        index = [slice(None) if b in open_bits else bits[b] for b in reversed(range(count))]
        return out_ref.at[tuple(index + [pl.ds(c * step, step)])]

    def add_groups(c):
        total = accs[-1][c, group].astype(f32)
        for d in range(1, groups):
            copies["z", c, d].wait_recv()
            total = total + recv_z[c, d - 1].astype(f32)
        place([], c)[...] = total.astype(jnp.bfloat16)

    def start_gather(c, stage):
        order = bit_order(c, count)[::-1]
        here = place(order[:stage], c)
        copies["g", c, stage] = send(
            here, here, gs.at[c, stage], gr.at[c, stage], partner(order[stage])
        )

    for c in range(chunks):
        start_scatter(c, 0)
    gain_w[0] = gain_ref[...]
    copies["x", 0] = send(gain_w.at[0], gain_w.at[count + 1], xs.at[0], xr.at[0], partner(0))

    for tick in range(chunks // 2 + 2 * count + 1):
        for c in range(chunks):
            s = tick - c // 2
            if 0 <= s < count:
                add_scatter(c, s)
                if s + 1 < count:
                    start_scatter(c, s + 1)
                else:
                    start_groups(c)
            elif s == count:
                add_groups(c)
                start_gather(c, 0)
            elif count < s <= 2 * count:
                copies["g", c, s - count - 1].wait_recv()
                if s < 2 * count:
                    start_gather(c, s - count)
        if tick < count:
            copies["x", tick].wait_recv()
            gain_w[tick + 1] = gain_w[tick] + gain_w[count + 1 + tick]
            if tick + 1 < count:
                copies["x", tick + 1] = send(
                    gain_w.at[tick + 1],
                    gain_w.at[count + 2 + tick],
                    xs.at[tick + 1],
                    xr.at[tick + 1],
                    partner(tick + 1),
                )
            else:
                gain_z[pl.ds(group, 1)] = gain_w[pl.ds(count, 1)]
                for d in range(1, groups):
                    copies["gz", d] = send(
                        gain_w.at[count],
                        gain_z.at[group],
                        gzs.at[d - 1],
                        gzr.at[d - 1],
                        (wide, (group + d) % groups),
                    )

    first = tuple([0] * count + [pl.ds(0, 16)])
    copies["h"] = send(out_ref.at[first], head_ref, hs, hr, (wide, (group + groups - 1) % groups))
    flat_lead = out_ref.shape[:-2]

    def squares(i, total):
        index = tuple((i // 2**b) % 2 for b in reversed(range(len(flat_lead))))
        value = out_ref[index].astype(f32)
        value = value * value
        return total + jnp.sum(value.reshape(-1, 8, LANES), axis=0)

    square = lax.fori_loop(0, math.prod(flat_lead), squares, jnp.zeros((8, LANES), f32))
    piece_head[...] = square
    sq_z[pl.ds(group, 1)] = square[None]
    for d in range(1, groups):
        copies["q", d] = send(
            piece_head, sq_z.at[group], qs.at[d - 1], qr.at[d - 1], (wide, (group + d) % groups)
        )
    for d in range(1, groups):
        copies["gz", d].wait_recv()
    gains = gain_z[0]
    for d in range(1, groups):
        gains = gains + gain_z[d]
    gsum_ref[...] = gains
    for d in range(1, groups):
        copies["q", d].wait_recv()
    square = sq_z[0]
    for d in range(1, groups):
        square = square + sq_z[d]
    sq_ref[...] = square
    copies["h"].wait_recv()
    for copy in copies.values():
        copy.wait_send()


def params_of(identity):
    return pltpu.CompilerParams(
        collective_id=identity, has_side_effects=True, vmem_limit_bytes=60 * 2**20
    )


def vmem_specs(n):
    return [pl.BlockSpec(memory_space=pltpu.VMEM)] * n


def gather_tails(tail, groups, identity):
    dma = pltpu.SemaphoreType.DMA
    return pl.pallas_call(
        functools.partial(tails_kernel, groups, 0),
        out_shape=jax.ShapeDtypeStruct((groups,) + tail.shape, tail.dtype),
        in_specs=vmem_specs(1),
        out_specs=vmem_specs(1)[0],
        scratch_shapes=[dma((groups - 1,)), dma((groups - 1,))],
        compiler_params=params_of(identity),
        name="tails",
    )(tail)


def gather_blocks(block, groups, count, chunks):
    dma = pltpu.SemaphoreType.DMA
    units = (groups - 1) * chunks
    return pl.pallas_call(
        functools.partial(gather_kernel, groups, count, chunks),
        out_shape=jax.ShapeDtypeStruct((groups,) + block.shape, block.dtype),
        in_specs=vmem_specs(1),
        out_specs=vmem_specs(1)[0],
        scratch_shapes=[
            dma,
            dma((units,)),
            dma((units,)),
            dma((units, count)),
            dma((units, count)),
        ],
        compiler_params=params_of(1),
        name="gather_weights",
    )(block)


def sum_blocks(main, gains, groups, count, chunks):
    dma = pltpu.SemaphoreType.DMA
    rows = main.shape[-2]
    step = rows // chunks
    bf16, f32 = jnp.bfloat16, jnp.float32
    stages = [
        pltpu.VMEM((chunks, groups) + (2,) * (count - 1 - k) + (step, LANES), bf16)
        for k in range(count)
    ]
    return pl.pallas_call(
        functools.partial(sum_kernel, groups, count, chunks),
        out_shape=(
            jax.ShapeDtypeStruct((2,) * count + (rows, LANES), bf16),
            jax.ShapeDtypeStruct((16, LANES), bf16),
            jax.ShapeDtypeStruct(gains.shape, f32),
            jax.ShapeDtypeStruct((8, LANES), f32),
        ),
        in_specs=vmem_specs(2),
        out_specs=tuple(vmem_specs(4)),
        scratch_shapes=stages
        + stages
        + [
            pltpu.VMEM((chunks, groups - 1, step, LANES), bf16),
            pltpu.VMEM((2 * count + 1,) + gains.shape, f32),
            pltpu.VMEM((groups,) + gains.shape, f32),
            pltpu.VMEM((groups, 8, LANES), f32),
            pltpu.VMEM((8, LANES), f32),
        ]
        + [dma((chunks, count))] * 2
        + [dma((chunks, groups - 1))] * 2
        + [dma((chunks, count))] * 2
        + [dma((count,))] * 2
        + [dma((groups - 1,))] * 4
        + [dma, dma],
        compiler_params=params_of(2),
        name="sum_grads",
    )(main, gains)


def dot(left_op, right_op, left_dim, right_dim):
    return lax.dot_general(
        left_op,
        right_op,
        (((left_dim,), (right_dim,)), ((), ())),
        preferred_element_type=jnp.float32,
    )


def layer_kernel(
    x_ref, seg_ref, cot_ref, w_ref, gain_ref, freq_ref,
    out_ref, din_ref, main_ref, gg_ref,
    att_s, mid_s, hid_s, down_s, dhid_s, dproj_s, dmid_s,
):
    f32, bf16 = jnp.float32, jnp.bfloat16
    width, length, half = MODEL_WIDTH, x_ref.shape[0], HEAD_SIZE // 2
    part = width // 2
    heads, kv = QUERY_HEADS, KEY_VALUE_HEADS
    repeat = heads // kv
    scale = HEAD_SIZE**-0.5
    first_panel = (heads * HEAD_SIZE) // LANES

    def zero_panel(p):
        return w_ref[0, pl.ds(p * width, width), :]

    def zero_pair(p):
        return jnp.concatenate([zero_panel(p), zero_panel(p + 1)], axis=-1)

    gain_one, gain_two = gain_ref[0:1, :], gain_ref[1:2, :]
    x = x_ref[...].astype(f32)
    inv_attn = lax.rsqrt(jnp.mean(x * x, axis=-1, keepdims=True) + norm_eps)
    normed_attn = x * inv_attn
    hidden_attn = (normed_attn * gain_one).astype(bf16)

    seg_row = jnp.broadcast_to(seg_ref[...].astype(f32), (length, length))
    rows = lax.broadcasted_iota(jnp.int32, (length, length), 0)
    columns = lax.broadcasted_iota(jnp.int32, (length, length), 1)
    allowed = (seg_row == seg_row.T) & (rows >= columns)
    positions = jnp.sum(jnp.where(allowed, 1.0, 0.0), axis=-1, keepdims=True) - 1.0
    angles = positions * freq_ref[...]
    lane = lax.broadcasted_iota(jnp.int32, (length, LANES), 1)
    first = lane % HEAD_SIZE < half
    cosine, sine = jnp.cos(angles), jnp.sin(angles)
    sine = jnp.where(first, -sine, sine)

    def swap(u):
        return jnp.where(first, pltpu.roll(u, LANES - half, 1), pltpu.roll(u, half, 1))

    plain = {}
    panels = 12
    for p in range(first_panel, panels, 2):
        both = dot(hidden_attn, zero_pair(p), 1, 0)
        plain[p], plain[p + 1] = both[:, :LANES], both[:, LANES:]
    turned = {p: u * cosine + swap(u) * sine for p, u in plain.items()}

    def slot(source, s):
        at = s % 2 * HEAD_SIZE
        return source[s // 2][:, at : at + HEAD_SIZE].astype(bf16)

    mask = jnp.concatenate([allowed] * repeat, axis=0)
    saved = []
    for j in range(kv):
        queries = jnp.concatenate([slot(turned, heads + repeat * j + r) for r in range(repeat)], axis=0)
        keys, values = slot(turned, 2 * heads + j), slot(plain, 2 * heads + kv + j)
        scores = jnp.where(mask, dot(queries, keys, 1, 1) * scale, masked_value)
        peak = jnp.max(scores, axis=-1, keepdims=True)
        total = jnp.sum(jnp.exp(scores - peak), axis=-1, keepdims=True)
        probs = jnp.exp(scores - (peak + jnp.log(total)))
        probs_b = probs.astype(bf16)
        attended = dot(probs_b, values, 1, 0)
        for r in range(repeat):
            at = (repeat * j + r) * HEAD_SIZE
            att_s[:, at : at + HEAD_SIZE] = attended[r * length : (r + 1) * length].astype(bf16)
        saved.append((queries, keys, values, probs, probs_b))

    attended = att_s[...]
    for p in range(0, first_panel, 2):
        at = p * LANES
        mid_s[:, at : at + 2 * LANES] = dot(attended, zero_pair(p), 1, 0)
    at = first_panel * LANES
    mid_s[:, at:width] = dot(attended, zero_panel(first_panel), 1, 0)[:, : width - at]
    mid = x + mid_s[...]
    inv_ffn = lax.rsqrt(jnp.mean(mid * mid, axis=-1, keepdims=True) + norm_eps)
    normed_ffn = mid * inv_ffn
    hid_s[...] = (normed_ffn * gain_two).astype(bf16)
    mid_s[...] = mid
    down_s[...] = jnp.zeros_like(down_s)
    dhid_s[...] = jnp.zeros_like(dhid_s)

    def gateup_rows(p):
        return pl.ds(pl.multiple_of(p * part, part), part)

    def gateup_pair(p):
        sides = [
            jnp.concatenate([w_ref[1, gateup_rows(q), :], w_ref[2, gateup_rows(q), :]], axis=0)
            for q in (p, p + 1)
        ]
        return jnp.concatenate(sides, axis=-1)

    def store_gateup(p, value):
        value = value.astype(bf16)
        for q in range(2):
            columns = slice(q * LANES, (q + 1) * LANES)
            main_ref[1, gateup_rows(p + q), :] = value[:part, columns]
            main_ref[2, gateup_rows(p + q), :] = value[part:, columns]

    half_panels = FF // LANES

    def hidden_step(i, _):
        p = 2 * i
        hidden, cotangent = hid_s[...], cot_ref[...]
        gate_w, up_w = gateup_pair(p), gateup_pair(p + half_panels)
        down_rows = [pl.ds(pl.multiple_of((p + q) * width, width), width) for q in range(2)]
        down_w = jnp.concatenate([w_ref[3, r, :] for r in down_rows], axis=-1)
        gate, upper = dot(hidden, gate_w, 1, 0), dot(hidden, up_w, 1, 0)
        d_act = dot(cotangent, down_w, 1, 0)
        sigmoid = jax.nn.sigmoid(gate)
        activation = (gate * sigmoid * upper).astype(bf16)
        d_gate = (d_act * upper * sigmoid * (1.0 + gate * (1.0 - sigmoid))).astype(bf16)
        d_upper = (d_act * gate * sigmoid).astype(bf16)
        down_s[...] += dot(activation, down_w, 1, 1)
        dhid_s[...] += dot(d_gate, gate_w, 1, 1) + dot(d_upper, up_w, 1, 1)
        store_gateup(p, dot(hidden, d_gate, 0, 0))
        store_gateup(p + half_panels, dot(hidden, d_upper, 0, 0))
        d_down = dot(cotangent, activation, 0, 0).astype(bf16)
        for q in range(2):
            main_ref[3, down_rows[q], :] = d_down[:, q * LANES : (q + 1) * LANES]
        return 0

    lax.fori_loop(0, half_panels // 2, hidden_step, 0)
    mid = mid_s[...]
    normed_ffn = mid * inv_ffn
    out_ref[...] = (mid + down_s[...]).astype(bf16)
    d_hidden = dhid_s[...]
    gg_ref[1:2, :] = jnp.sum(d_hidden * normed_ffn, axis=0, keepdims=True)
    d_mid = cot_ref[...].astype(f32) + norm_back(d_hidden, normed_ffn, inv_ffn, gain_two)
    dmid_s[...] = jnp.zeros_like(dmid_s)
    dmid_s[:, :width] = d_mid.astype(bf16)
    attended = att_s[...]
    d_attended = jnp.zeros((length, width), f32)
    for p in range(0, first_panel + 2, 2):
        at = p * LANES
        if p == first_panel:
            block = dmid_s[:, at : at + LANES]
            d_attended += dot(block, zero_panel(p), 1, 1)
        else:
            block = dmid_s[:, at : at + 2 * LANES]
            d_attended += dot(block, zero_pair(p), 1, 1)
        value = dot(attended, block, 0, 0)
        if p == first_panel:
            edge = value
        else:
            main_ref[0, pl.ds(p * width, width), :] = value[:, :LANES].astype(bf16)
            main_ref[0, pl.ds((p + 1) * width, width), :] = value[:, LANES:].astype(bf16)
    att_s[...] = d_attended.astype(bf16)

    dproj_s[...] = jnp.zeros_like(dproj_s)
    start = first_panel * 2
    for j in range(kv):
        queries, keys, values, probs, probs_b = saved[j]
        d_att = jnp.concatenate(
            [
                att_s[:, (repeat * j + r) * HEAD_SIZE : (repeat * j + r + 1) * HEAD_SIZE]
                for r in range(repeat)
            ],
            axis=0,
        )
        d_probs = dot(d_att, values, 1, 1)
        row_total = jnp.sum(probs * d_probs, axis=-1, keepdims=True)
        d_scores = (probs * (d_probs - row_total) * scale).astype(bf16)
        d_queries = dot(d_scores, keys, 1, 0)
        for r in range(repeat):
            at = (heads + repeat * j + r - start) * HEAD_SIZE
            dproj_s[:, at : at + HEAD_SIZE] = d_queries[r * length : (r + 1) * length]
        at = (2 * heads + j - start) * HEAD_SIZE
        dproj_s[:, at : at + HEAD_SIZE] = dot(d_scores, queries, 0, 0)
        at = (2 * heads + kv + j - start) * HEAD_SIZE
        dproj_s[:, at : at + HEAD_SIZE] = dot(probs_b, d_att, 0, 0)

    turned_lanes = (2 * heads + kv - start) * HEAD_SIZE
    d_hidden = jnp.zeros((length, width), f32)
    for p in range(first_panel, panels, 2):
        sides = []
        for q in (p, p + 1):
            at = (q - first_panel) * LANES
            raw = dproj_s[:, at : at + LANES]
            back = raw * cosine - swap(raw) * sine
            sides.append(jnp.where(lane + at < turned_lanes, back, raw).astype(bf16))
        both = jnp.concatenate(sides, axis=-1)
        d_hidden += dot(both, zero_pair(p), 1, 1)
        value = dot(hidden_attn, both, 0, 0)
        left = value[:, :LANES]
        if p == first_panel:
            left = left + edge
        main_ref[0, pl.ds(p * width, width), :] = left.astype(bf16)
        main_ref[0, pl.ds((p + 1) * width, width), :] = value[:, LANES:].astype(bf16)
    gg_ref[0:1, :] = jnp.sum(d_hidden * normed_attn, axis=0, keepdims=True)
    din_ref[...] = (d_mid + norm_back(d_hidden, normed_attn, inv_attn, gain_one)).astype(bf16)


def layer_panels(inputs, segment_row, cotangent, weights, gains):
    length = inputs.shape[0]
    half = HEAD_SIZE // 2
    f32, bf16 = jnp.float32, jnp.bfloat16
    freqs = theta_base ** (-2.0 * jnp.arange(half, dtype=f32) / HEAD_SIZE)
    freqs = jnp.tile(freqs, LANES // half)[None]
    full = (length, MODEL_WIDTH)
    kept = (QUERY_HEADS * HEAD_SIZE) // LANES * LANES
    return pl.pallas_call(
        layer_kernel,
        out_shape=(
            jax.ShapeDtypeStruct(full, bf16),
            jax.ShapeDtypeStruct(full, bf16),
            jax.ShapeDtypeStruct(weights.shape, bf16),
            jax.ShapeDtypeStruct((2, MODEL_WIDTH), f32),
        ),
        in_specs=vmem_specs(6),
        out_specs=tuple(vmem_specs(4)),
        scratch_shapes=[
            pltpu.VMEM(full, bf16),
            pltpu.VMEM(full, f32),
            pltpu.VMEM(full, bf16),
            pltpu.VMEM(full, f32),
            pltpu.VMEM(full, f32),
            pltpu.VMEM((length, FF - kept), f32),
            pltpu.VMEM((length, kept + LANES), bf16),
        ],
        compiler_params=pltpu.CompilerParams(vmem_limit_bytes=60 * 2**20),
        name="layer",
    )(inputs, segment_row[None], cotangent, weights, gains.astype(f32).reshape(2, MODEL_WIDTH), freqs)


def columns_to_panels(matrix):
    return matrix.reshape(matrix.shape[0], -1, LANES).swapaxes(0, 1).reshape(-1, LANES)


def panels_to_columns(panels, rows):
    return panels.reshape(-1, rows, LANES).swapaxes(0, 1).reshape(rows, -1)


def block_to_panels(flat, group):
    inner = QUERY_HEADS * HEAD_SIZE
    qkv = inner + 2 * KEY_VALUE_HEADS * HEAD_SIZE
    cut = MODEL_WIDTH * qkv

    def joint(v):
        out, w = v[cut:].reshape(inner, MODEL_WIDTH), v[:cut].reshape(MODEL_WIDTH, qkv)
        return columns_to_panels(jnp.concatenate([out, w], axis=1))

    def gateup(v):
        return columns_to_panels(v.reshape(-1, 2 * FF))

    def down(v):
        return columns_to_panels(v.reshape(FF, MODEL_WIDTH).T)

    return lax.switch(group, [joint, gateup, gateup, down], flat)


def panels_to_block(panels, group):
    inner = QUERY_HEADS * HEAD_SIZE

    def joint(v):
        both = panels_to_columns(v, MODEL_WIDTH)
        return jnp.concatenate([both[:, MODEL_WIDTH:].reshape(-1), both[:, :MODEL_WIDTH].reshape(-1)])

    def gateup(v):
        return panels_to_columns(v, MODEL_WIDTH // 2).reshape(-1)

    def down(v):
        return panels_to_columns(v, MODEL_WIDTH).T.reshape(-1)

    return lax.switch(group, [joint, gateup, gateup, down], panels)


def on_device(inputs, segments, cotangent, params, moment_one, moment_two):
    groups = lax.axis_size("group")
    wides = lax.axis_size("wide")
    group = lax.axis_index("group")
    count = wides.bit_length() - 1
    share_len = params.shape[0]
    gain_len = 2 * MODEL_WIDTH
    extra = gain_len // groups
    block_len = share_len - extra
    block_rows = block_len // LANES
    piece_rows = -(-block_rows // wides)
    chunks = 6 if piece_rows % 96 == 0 else 2
    piece_rows = -(-piece_rows // (16 * chunks)) * 16 * chunks
    padding = piece_rows * wides - block_rows
    lead = (2,) * count

    def to_pieces(rows):
        rows = rows.reshape(-1, block_rows, LANES)
        if padding:
            rows = jnp.pad(rows, ((0, 0), (0, padding), (0, 0)))
        return rows.reshape((-1,) + lead + (piece_rows, LANES))

    def from_pieces(pieces):
        rows = pieces.reshape(-1, piece_rows * wides, LANES)[:, :block_rows]
        return rows.reshape(-1, LANES)

    rounded = params.astype(jnp.bfloat16)
    tail = jnp.pad(rounded[share_len - gain_len :], (0, 16 * LANES - gain_len)).reshape(16, LANES)
    tails = gather_tails(tail, groups, 0).reshape(groups, -1)[:, :gain_len]
    before = lax.dynamic_index_in_dim(tails, (group + groups - 1) % groups, keepdims=False)
    joined = jnp.concatenate([before, rounded])
    block = lax.dynamic_slice(joined, (gain_len - extra * group,), (block_len,))
    by_panels = groups == 4 and block_len == MODEL_WIDTH * FF and not padding
    flat_gains = tails[groups - 1]
    if by_panels:
        block = block_to_panels(block, group)
        gathered = gather_blocks(to_pieces(block)[0], groups, count, 2)
        outputs, d_inputs, main, gains = layer_panels(
            inputs[0],
            segments[0],
            cotangent[0],
            gathered.reshape(groups, block_rows, LANES),
            flat_gains,
        )
        gains = gains.reshape(-1)
    else:
        gathered = gather_blocks(to_pieces(block)[0], groups, count, 2)
        weights = unpack(from_pieces(gathered), flat_gains)
        outputs, d_inputs, main, gains = layer_row(inputs[0], segments[0], cotangent[0], weights)
    gains = gains.astype(jnp.bfloat16).astype(jnp.float32)
    gains = jnp.pad(gains, (0, 16 * LANES - gain_len)).reshape(16, LANES)
    summed_block, head, gains, square = sum_blocks(to_pieces(main), gains, groups, count, chunks)
    gains = gains.reshape(-1)[:gain_len].astype(jnp.bfloat16)
    if by_panels:
        flat_block = panels_to_block(from_pieces(summed_block), group)
        head = jnp.pad(flat_block[:gain_len], (0, 16 * LANES - gain_len)).reshape(16, LANES)
        heads = gather_tails(head, groups, 3).reshape(groups, -1)[:, :gain_len]
        head = lax.dynamic_index_in_dim(heads, (group + 1) % groups, keepdims=False)
    else:
        flat_block = from_pieces(summed_block).reshape(-1)
        head = head.reshape(-1)[:gain_len]
    head = jnp.where(group == groups - 1, gains, head)
    joined = jnp.concatenate([flat_block, head])
    summed = lax.dynamic_slice(joined, (extra * group,), (share_len,)).astype(jnp.float32)
    gains = gains.astype(jnp.float32)
    squares = jnp.sum(square) + jnp.sum(gains * gains)
    clip_factor = jnp.minimum(jnp.float32(1.0), max_norm * lax.rsqrt(squares))
    flat_index = group * share_len + jnp.arange(share_len, dtype=jnp.int32)
    decay_mask = flat_index < share_len * groups - gain_len
    new_params, new_moment_one, new_moment_two = adam_update(
        summed, clip_factor, params, moment_one, moment_two, decay_mask
    )
    return (outputs[None], d_inputs[None], summed, new_params, new_moment_one, new_moment_two)


def solution(mesh):
    return jax.shard_map(
        on_device,
        mesh=mesh,
        in_specs=(
            P(("wide", "group"), None, None),
            P(("wide", "group"), None),
            P(("wide", "group"), None, None),
            P("group"),
            P("group"),
            P("group"),
        ),
        out_specs=(
            P(("wide", "group"), None, None),
            P(("wide", "group"), None, None),
            P("group"),
            P("group"),
            P("group"),
            P("group"),
        ),
        check_vma=False,
    )
```

```python
import functools
import math

import jax
import jax.numpy as jnp
from jax import lax
from jax.experimental import pallas as pl
from jax.experimental.pallas import tpu as pltpu
from jax.sharding import PartitionSpec as P

MESH = pl.DeviceIdType.MESH
LANES = 128

MODEL_WIDTH = 576
QUERY_HEADS = 9
KEY_VALUE_HEADS = 3
HEAD_SIZE = 64
FF = 1536


norm_eps = 1e-05
theta_base = 10000.0
masked_value = -1e30
beta_one = 0.9
beta_two = 0.95
bias_one = 0.19
bias_two = 0.0975
learn_rate = 0.03
decay_rate = 0.1
adam_eps = 1e-08
max_norm = 1.0


def contract(pattern, left_op, right_op):
    return jnp.einsum(pattern, left_op, right_op, preferred_element_type=jnp.float32)


def inner_rows(left_op, right_op):
    return lax.dot_general(
        left_op, right_op, (((0,), (0,)), ((), ())), preferred_element_type=jnp.float32
    )


def outer_column_count(left_op, right_op):
    return lax.dot_general(
        left_op, right_op, (((1,), (1,)), ((), ())), preferred_element_type=jnp.float32
    )


def unpack(main, gains):
    query_key_value_width = (QUERY_HEADS + 2 * KEY_VALUE_HEADS) * HEAD_SIZE
    shapes = [
        (MODEL_WIDTH, query_key_value_width),
        (QUERY_HEADS * HEAD_SIZE, MODEL_WIDTH),
        (MODEL_WIDTH, 2 * FF),
        (FF, MODEL_WIDTH),
    ]
    pieces = []
    offset = 0
    for piece_shape in shapes:
        extent = math.prod(piece_shape) // LANES
        pieces.append(main[offset : offset + extent].reshape(piece_shape))
        offset += extent
    return pieces + [gains[:MODEL_WIDTH], gains[MODEL_WIDTH:]]


def positions_of(segment_row):
    index_row = jnp.arange(segment_row.shape[0], dtype=jnp.int32)
    previous = jnp.concatenate([segment_row[:1] - 1, segment_row[:-1]])
    starts = jnp.where(segment_row != previous, index_row, jnp.zeros_like(index_row))
    return index_row - lax.cummax(starts, axis=0)


def rope_tables(positions):
    half_size = HEAD_SIZE // 2
    freqs = theta_base ** (-2.0 * jnp.arange(half_size, dtype=jnp.float32) / HEAD_SIZE)
    angles = positions.astype(jnp.float32)[:, None] * freqs[None, :]
    return (jnp.cos(angles)[:, None, :], jnp.sin(angles)[:, None, :])


def apply_rotation(vectors, cosine_lookup, sine_lookup):
    half_size = HEAD_SIZE // 2
    first_half = vectors[..., :half_size]
    second_half = vectors[..., half_size:]
    return jnp.concatenate(
        [
            first_half * cosine_lookup - second_half * sine_lookup,
            second_half * cosine_lookup + first_half * sine_lookup,
        ],
        axis=-1,
    )


def unrotate(vectors, cosine_lookup, sine_lookup):
    half_size = HEAD_SIZE // 2
    first_half = vectors[..., :half_size]
    second_half = vectors[..., half_size:]
    return jnp.concatenate(
        [
            first_half * cosine_lookup + second_half * sine_lookup,
            second_half * cosine_lookup - first_half * sine_lookup,
        ],
        axis=-1,
    )


def norm_back(d_hidden, normed, inverse, gain):
    d_normed = d_hidden * gain
    return inverse * (d_normed - normed * jnp.mean(d_normed * normed, axis=-1, keepdims=True))


def layer_row(inputs, segment_row, cotangent, weights):
    query_key_value_weight, output_weight, w_gateup, w_down, gain_attn, gain_ffn = weights
    sequence_length = inputs.shape[0]
    repeat_count = QUERY_HEADS // KEY_VALUE_HEADS
    scale_factor = HEAD_SIZE ** (-0.5)
    gain_one = gain_attn.astype(jnp.float32)
    gain_two = gain_ffn.astype(jnp.float32)
    resid_in = inputs.astype(jnp.float32)
    inv_attn = lax.rsqrt(jnp.mean(resid_in * resid_in, axis=-1, keepdims=True) + norm_eps)
    normed_attn = resid_in * inv_attn
    hidden_attn = (normed_attn * gain_one).astype(jnp.bfloat16)
    projected_output = jnp.dot(
        hidden_attn, query_key_value_weight, preferred_element_type=jnp.float32
    )
    cosine_lookup, sine_lookup = rope_tables(positions_of(segment_row))
    query_rows = projected_output[:, : QUERY_HEADS * HEAD_SIZE].reshape(
        sequence_length, QUERY_HEADS, HEAD_SIZE
    )
    key_matrix = projected_output[
        :, QUERY_HEADS * HEAD_SIZE : (QUERY_HEADS + KEY_VALUE_HEADS) * HEAD_SIZE
    ].reshape(sequence_length, KEY_VALUE_HEADS, HEAD_SIZE)
    query_rows_rotated = (
        apply_rotation(query_rows, cosine_lookup, sine_lookup)
        .astype(jnp.bfloat16)
        .reshape(sequence_length, KEY_VALUE_HEADS, repeat_count, HEAD_SIZE)
    )
    keys_rot = apply_rotation(key_matrix, cosine_lookup, sine_lookup).astype(jnp.bfloat16)
    value_rows = (
        projected_output[:, (QUERY_HEADS + KEY_VALUE_HEADS) * HEAD_SIZE :]
        .reshape(sequence_length, KEY_VALUE_HEADS, HEAD_SIZE)
        .astype(jnp.bfloat16)
    )
    index_row = jnp.arange(sequence_length)
    allowed = (segment_row[:, None] == segment_row[None, :]) & (
        index_row[:, None] >= index_row[None, :]
    )
    scores = contract("qgrd,kgd->grqk", query_rows_rotated, keys_rot) * scale_factor
    scores = jnp.where(allowed, scores, masked_value)
    peak = jnp.max(scores, axis=-1, keepdims=True)
    log_total = peak + jnp.log(jnp.sum(jnp.exp(scores - peak), axis=-1, keepdims=True))
    probs_b = jnp.exp(scores - log_total).astype(jnp.bfloat16)
    attended = (
        contract("grqk,kgd->qgrd", probs_b, value_rows)
        .astype(jnp.bfloat16)
        .reshape(sequence_length, QUERY_HEADS * HEAD_SIZE)
    )
    mid = resid_in + jnp.dot(attended, output_weight, preferred_element_type=jnp.float32)
    inv_ffn = lax.rsqrt(jnp.mean(mid * mid, axis=-1, keepdims=True) + norm_eps)
    normed_ffn = mid * inv_ffn
    hidden_ffn = (normed_ffn * gain_two).astype(jnp.bfloat16)
    gate_up = jnp.dot(hidden_ffn, w_gateup, preferred_element_type=jnp.float32)
    gate_pre = gate_up[:, :FF]
    upper = gate_up[:, FF:]
    sigmoid_gate = jax.nn.sigmoid(gate_pre)
    activation = (gate_pre * sigmoid_gate * upper).astype(jnp.bfloat16)
    outputs = (mid + jnp.dot(activation, w_down, preferred_element_type=jnp.float32)).astype(
        jnp.bfloat16
    )
    grad_down = inner_rows(activation, cotangent)
    d_act = outer_column_count(cotangent, w_down)
    d_gate = d_act * upper * sigmoid_gate * (1.0 + gate_pre * (1.0 - sigmoid_gate))
    d_upper = d_act * gate_pre * sigmoid_gate
    d_gate_up = jnp.concatenate([d_gate, d_upper], axis=-1).astype(jnp.bfloat16)
    grad_gateup = inner_rows(hidden_ffn, d_gate_up)
    d_hidden_ffn = outer_column_count(d_gate_up, w_gateup)
    grad_gain_ffn = jnp.sum(d_hidden_ffn * normed_ffn, axis=0)
    d_mid = cotangent.astype(jnp.float32) + norm_back(d_hidden_ffn, normed_ffn, inv_ffn, gain_two)
    grad_middle_batch = d_mid.astype(jnp.bfloat16)
    grad_out = inner_rows(attended, grad_middle_batch)
    grad_attended_rows = (
        outer_column_count(grad_middle_batch, output_weight)
        .astype(jnp.bfloat16)
        .reshape(sequence_length, KEY_VALUE_HEADS, repeat_count, HEAD_SIZE)
    )
    recomputed = contract("qgrd,kgd->grqk", query_rows_rotated, keys_rot) * scale_factor
    probs = jnp.exp(jnp.where(allowed, recomputed, masked_value) - log_total)
    d_probs = contract("qgrd,kgd->grqk", grad_attended_rows, value_rows)
    row_total = jnp.sum(probs * d_probs, axis=-1, keepdims=True)
    d_scores = (probs * (d_probs - row_total) * scale_factor).astype(jnp.bfloat16)
    grad_query_rows = contract("grqk,kgd->qgrd", d_scores, keys_rot).reshape(
        sequence_length, QUERY_HEADS, HEAD_SIZE
    )
    grad_key_rows = contract("grqk,qgrd->kgd", d_scores, query_rows_rotated)
    grad_value_rows = contract("grqk,qgrd->kgd", probs_b, grad_attended_rows)
    grad_query_rows = unrotate(grad_query_rows, cosine_lookup, sine_lookup)
    grad_key_rows = unrotate(grad_key_rows, cosine_lookup, sine_lookup)
    grad_projected_rows = jnp.concatenate(
        [
            grad_query_rows.reshape(sequence_length, QUERY_HEADS * HEAD_SIZE),
            grad_key_rows.reshape(sequence_length, KEY_VALUE_HEADS * HEAD_SIZE),
            grad_value_rows.reshape(sequence_length, KEY_VALUE_HEADS * HEAD_SIZE),
        ],
        axis=-1,
    ).astype(jnp.bfloat16)
    grad_qkv = inner_rows(hidden_attn, grad_projected_rows)
    d_hidden_attn = outer_column_count(grad_projected_rows, query_key_value_weight)
    grad_gain_attn = jnp.sum(d_hidden_attn * normed_attn, axis=0)
    d_inputs = (d_mid + norm_back(d_hidden_attn, normed_attn, inv_attn, gain_one)).astype(
        jnp.bfloat16
    )
    matrices = [grad_qkv, grad_out, grad_gateup, grad_down]
    main = jnp.concatenate([m.astype(jnp.bfloat16).reshape(-1, LANES) for m in matrices])
    gains = jnp.concatenate([grad_gain_attn, grad_gain_ffn])
    return (outputs, d_inputs, main, gains)


def adam_update(grads, clip_factor, params, moment_one, moment_two, decay_mask):
    clipped = grads * clip_factor
    new_moment_one = beta_one * moment_one + (1.0 - beta_one) * clipped
    new_moment_two = beta_two * moment_two + (1.0 - beta_two) * clipped * clipped
    step_size = new_moment_one / bias_one / (jnp.sqrt(new_moment_two / bias_two) + adam_eps)
    decay_term = jnp.where(decay_mask, decay_rate * params, jnp.zeros_like(params))
    new_params = params - learn_rate * (step_size + decay_term)
    return (new_params, new_moment_one, new_moment_two)


def my_bits(wide, count):
    return [(wide // 2**b) % 2 for b in range(count)]


def flipped(wide, bit, b):
    return wide + (1 - 2 * bit) * 2**b


def greet(wide, group, bits, groups):
    barrier = pltpu.get_barrier_semaphore()
    peers = [(flipped(wide, bit, b), group) for b, bit in enumerate(bits)]
    peers += [(wide, (group + d) % groups) for d in range(1, groups)]
    for peer in peers:
        pl.semaphore_signal(barrier, inc=1, device_id=peer, device_id_type=MESH)
    pl.semaphore_wait(barrier, len(peers))


def send(src, dst, send_sem, recv_sem, peer):
    copy = pltpu.make_async_remote_copy(
        src_ref=src,
        dst_ref=dst,
        send_sem=send_sem,
        recv_sem=recv_sem,
        device_id=peer,
        device_id_type=MESH,
    )
    copy.start()
    return copy


def bit_order(chunk, count):
    rest = list(range(1, count))
    return [0] + (rest if chunk % 2 == 0 else rest[::-1])


def tails_kernel(groups, bits_count, tail_ref, out_ref, send_sem, recv_sem):
    wide, group = lax.axis_index("wide"), lax.axis_index("group")
    greet(wide, group, [], groups)
    out_ref[pl.ds(group, 1)] = tail_ref[...][None]
    copies = []
    for d in range(1, groups):
        copies.append(
            send(
                tail_ref,
                out_ref.at[group],
                send_sem.at[d - 1],
                recv_sem.at[d - 1],
                (wide, (group + d) % groups),
            )
        )
    for copy in copies:
        copy.wait()


def gather_kernel(groups, count, chunks, block_ref, out_ref, own_sem, zs, zr, ws, wr):
    wide, group = lax.axis_index("wide"), lax.axis_index("group")
    bits = my_bits(wide, count)
    step = block_ref.shape[-2] // chunks
    greet(wide, group, bits, groups)

    def place(ref, lead, open_bits, chunk):
        index = [slice(None) if b in open_bits else bits[b] for b in reversed(range(count))]
        return ref.at[tuple(lead + index + [pl.ds(chunk * step, step)])]

    def copy(src, dst, send_sem, recv_sem, peer):
        return pltpu.make_async_remote_copy(
            src_ref=src,
            dst_ref=dst,
            send_sem=send_sem,
            recv_sem=recv_sem,
            device_id=peer,
            device_id_type=MESH,
        )

    def along(way, d, c):
        source = (group - way * (d - 1) + groups) % groups
        unit = (0 if way > 0 else groups - 1) + d - 1
        src = place(block_ref, [], [], c) if d == 1 else place(out_ref, [source], [], c)
        return copy(
            src,
            place(out_ref, [source], [], c),
            zs.at[unit, c],
            zr.at[unit, c],
            (wide, (group + way + groups) % groups),
        )

    def passes(way, d):
        ahead = group + way
        behind = group - way * (d - 1)
        return (ahead >= 0) & (ahead < groups) & (behind >= 0) & (behind < groups)

    def comes(way, d):
        behind = group - way * d
        return (behind >= 0) & (behind < groups)

    def across(way, d, c, stage):
        order = bit_order(c, count)[::-1]
        b = order[stage]
        source = (group - way * d + groups) % groups
        unit = (0 if way > 0 else groups - 1) + d - 1
        here = place(out_ref, [source], order[:stage], c)
        return copy(
            here,
            here,
            ws.at[unit, c, stage],
            wr.at[unit, c, stage],
            (flipped(wide, bits[b], b), group),
        )

    units = [(d, c) for d in range(1, groups) for c in range(chunks)]
    for c in range(chunks):
        for way in (1, -1):

            @pl.when(passes(way, 1))
            def _():
                along(way, 1, c).start()

    own = pltpu.make_async_copy(block_ref, out_ref.at[group], own_sem)
    own.start()
    for tick in range(len(units) // 2 + count + 1):
        for u, (d, c) in reversed(list(enumerate(units))):
            stage = tick - u // 2
            if not 0 <= stage <= count:
                continue
            for way in (1, -1):

                @pl.when(comes(way, d))
                def _():
                    if stage == 0:
                        along(way, d, c).wait_recv()
                    else:
                        across(way, d, c, stage - 1).wait_recv()
                    if stage < count:
                        across(way, d, c, stage).start()

                if stage == 0 and d + 1 < groups:

                    @pl.when(passes(way, d + 1))
                    def _():
                        along(way, d + 1, c).start()

    for way in (1, -1):
        for d, c in units:

            @pl.when(passes(way, d))
            def _():
                along(way, d, c).wait_send()

            @pl.when(comes(way, d))
            def _():
                for stage in range(count):
                    across(way, d, c, stage).wait_send()

    own.wait()


def sum_kernel(groups, count, chunks, x_ref, gain_ref, out_ref, head_ref, gsum_ref, sq_ref, *scratch):
    recvs, accs = scratch[:count], scratch[count : 2 * count]
    recv_z, gain_w, gain_z, sq_z, piece_head = scratch[2 * count : 2 * count + 5]
    ss, sr, zs, zr, gs, gr, xs, xr, gzs, gzr, qs, qr, hs, hr = scratch[2 * count + 5 :]
    wide, group = lax.axis_index("wide"), lax.axis_index("group")
    bits = my_bits(wide, count)
    step = x_ref.shape[-2] // chunks
    greet(wide, group, bits, groups)
    copies = {}
    f32 = jnp.float32

    def partner(b):
        return (flipped(wide, bits[b], b), group)

    def part(c, stage, value):
        order = bit_order(c, count)
        left = sorted(order[stage:], reverse=True)
        return [value if b == order[stage] else slice(None) for b in left]

    def held(c, stage):
        return x_ref if stage == 0 else accs[stage - 1].at[c]

    def view(c, stage, flip):
        b = bit_order(c, count)[stage]
        index = [slice(None)] + part(c, stage, 1 - bits[b] if flip else bits[b])
        if stage == 0:
            index += [slice(None)] * (count + 2 - len(index) - 1)
            return x_ref.at[tuple(index + [pl.ds(c * step, step)])]
        return accs[stage - 1].at[tuple([c] + index)]

    def start_scatter(c, stage):
        b = bit_order(c, count)[stage]
        copies["s", c, stage] = send(
            view(c, stage, True), recvs[stage].at[c], ss.at[c, stage], sr.at[c, stage], partner(b)
        )

    def add_scatter(c, stage):
        copies["s", c, stage].wait_recv()
        mine, other, total = view(c, stage, False), recvs[stage].at[c], accs[stage].at[c]

        def body(i, _):
            total[i] = (mine[i].astype(f32) + other[i].astype(f32)).astype(jnp.bfloat16)
            return 0

        lax.fori_loop(0, groups, body, 0)

    def start_groups(c):
        for d in range(1, groups):
            to = (group + d) % groups
            copies["z", c, d] = send(
                accs[-1].at[c, to],
                recv_z.at[c, d - 1],
                zs.at[c, d - 1],
                zr.at[c, d - 1],
                (wide, to),
            )

    def place(open_bits, c):
        index = [slice(None) if b in open_bits else bits[b] for b in reversed(range(count))]
        return out_ref.at[tuple(index + [pl.ds(c * step, step)])]

    def add_groups(c):
        total = accs[-1][c, group].astype(f32)
        for d in range(1, groups):
            copies["z", c, d].wait_recv()
            total = total + recv_z[c, d - 1].astype(f32)
        place([], c)[...] = total.astype(jnp.bfloat16)

    def start_gather(c, stage):
        order = bit_order(c, count)[::-1]
        here = place(order[:stage], c)
        copies["g", c, stage] = send(
            here, here, gs.at[c, stage], gr.at[c, stage], partner(order[stage])
        )

    for c in range(chunks):
        start_scatter(c, 0)
    gain_w[0] = gain_ref[...]
    copies["x", 0] = send(gain_w.at[0], gain_w.at[count + 1], xs.at[0], xr.at[0], partner(0))

    for tick in range(chunks // 2 + 2 * count + 1):
        for c in range(chunks):
            s = tick - c // 2
            if 0 <= s < count:
                add_scatter(c, s)
                if s + 1 < count:
                    start_scatter(c, s + 1)
                else:
                    start_groups(c)
            elif s == count:
                add_groups(c)
                start_gather(c, 0)
            elif count < s <= 2 * count:
                copies["g", c, s - count - 1].wait_recv()
                if s < 2 * count:
                    start_gather(c, s - count)
        if tick < count:
            copies["x", tick].wait_recv()
            gain_w[tick + 1] = gain_w[tick] + gain_w[count + 1 + tick]
            if tick + 1 < count:
                copies["x", tick + 1] = send(
                    gain_w.at[tick + 1],
                    gain_w.at[count + 2 + tick],
                    xs.at[tick + 1],
                    xr.at[tick + 1],
                    partner(tick + 1),
                )
            else:
                gain_z[pl.ds(group, 1)] = gain_w[pl.ds(count, 1)]
                for d in range(1, groups):
                    copies["gz", d] = send(
                        gain_w.at[count],
                        gain_z.at[group],
                        gzs.at[d - 1],
                        gzr.at[d - 1],
                        (wide, (group + d) % groups),
                    )

    first = tuple([0] * count + [pl.ds(0, 16)])
    copies["h"] = send(out_ref.at[first], head_ref, hs, hr, (wide, (group + groups - 1) % groups))
    flat_lead = out_ref.shape[:-2]

    def squares(i, total):
        index = tuple((i // 2**b) % 2 for b in reversed(range(len(flat_lead))))
        value = out_ref[index].astype(f32)
        value = value * value
        return total + jnp.sum(value.reshape(-1, 8, LANES), axis=0)

    square = lax.fori_loop(0, math.prod(flat_lead), squares, jnp.zeros((8, LANES), f32))
    piece_head[...] = square
    sq_z[pl.ds(group, 1)] = square[None]
    for d in range(1, groups):
        copies["q", d] = send(
            piece_head, sq_z.at[group], qs.at[d - 1], qr.at[d - 1], (wide, (group + d) % groups)
        )
    for d in range(1, groups):
        copies["gz", d].wait_recv()
    gains = gain_z[0]
    for d in range(1, groups):
        gains = gains + gain_z[d]
    gains = gains.astype(jnp.bfloat16).astype(f32)
    gsum_ref[...] = gains
    for d in range(1, groups):
        copies["q", d].wait_recv()
    square = sq_z[0]
    for d in range(1, groups):
        square = square + sq_z[d]
    square = square + jnp.sum((gains * gains).reshape(-1, 8, LANES), axis=0)
    total = jnp.sum(jnp.sum(square, axis=-1, keepdims=True), axis=0, keepdims=True)
    clip = jnp.minimum(jnp.float32(1.0), max_norm * lax.rsqrt(total))
    sq_ref[...] = jnp.broadcast_to(clip, sq_ref.shape)
    copies["h"].wait_recv()
    for copy in copies.values():
        copy.wait_send()


def params_of(identity):
    return pltpu.CompilerParams(
        collective_id=identity, has_side_effects=True, vmem_limit_bytes=60 * 2**20
    )


def vmem_specs(n):
    return [pl.BlockSpec(memory_space=pltpu.VMEM)] * n


def gather_tails(tail, groups, identity):
    dma = pltpu.SemaphoreType.DMA
    return pl.pallas_call(
        functools.partial(tails_kernel, groups, 0),
        out_shape=jax.ShapeDtypeStruct((groups,) + tail.shape, tail.dtype),
        in_specs=vmem_specs(1),
        out_specs=vmem_specs(1)[0],
        scratch_shapes=[dma((groups - 1,)), dma((groups - 1,))],
        compiler_params=params_of(identity),
        name="tails",
    )(tail)


def gather_blocks(block, groups, count, chunks):
    dma = pltpu.SemaphoreType.DMA
    units = 2 * (groups - 1)
    return pl.pallas_call(
        functools.partial(gather_kernel, groups, count, chunks),
        out_shape=jax.ShapeDtypeStruct((groups,) + block.shape, block.dtype),
        in_specs=vmem_specs(1),
        out_specs=vmem_specs(1)[0],
        scratch_shapes=[
            dma,
            dma((units, chunks)),
            dma((units, chunks)),
            dma((units, chunks, count)),
            dma((units, chunks, count)),
        ],
        compiler_params=params_of(1),
        name="gather_weights",
    )(block)


def sum_blocks(main, gains, groups, count, chunks):
    dma = pltpu.SemaphoreType.DMA
    rows = main.shape[-2]
    step = rows // chunks
    bf16, f32 = jnp.bfloat16, jnp.float32
    stages = [
        pltpu.VMEM((chunks, groups) + (2,) * (count - 1 - k) + (step, LANES), bf16)
        for k in range(count)
    ]
    return pl.pallas_call(
        functools.partial(sum_kernel, groups, count, chunks),
        out_shape=(
            jax.ShapeDtypeStruct((2,) * count + (rows, LANES), bf16),
            jax.ShapeDtypeStruct((16, LANES), bf16),
            jax.ShapeDtypeStruct(gains.shape, f32),
            jax.ShapeDtypeStruct((8, LANES), f32),
        ),
        in_specs=vmem_specs(2),
        out_specs=tuple(vmem_specs(4)),
        scratch_shapes=stages
        + stages
        + [
            pltpu.VMEM((chunks, groups - 1, step, LANES), bf16),
            pltpu.VMEM((2 * count + 1,) + gains.shape, f32),
            pltpu.VMEM((groups,) + gains.shape, f32),
            pltpu.VMEM((groups, 8, LANES), f32),
            pltpu.VMEM((8, LANES), f32),
        ]
        + [dma((chunks, count))] * 2
        + [dma((chunks, groups - 1))] * 2
        + [dma((chunks, count))] * 2
        + [dma((count,))] * 2
        + [dma((groups - 1,))] * 4
        + [dma, dma],
        compiler_params=params_of(2),
        name="sum_grads",
    )(main, gains)


def dot(left_op, right_op, left_dim, right_dim):
    return lax.dot_general(
        left_op,
        right_op,
        (((left_dim,), (right_dim,)), ((), ())),
        preferred_element_type=jnp.float32,
    )


def layer_kernel(
    x_ref, seg_ref, cot_ref, w_ref, gain_ref, freq_ref,
    out_ref, din_ref, main_ref, gg_ref,
    att_s, mid_s, hid_s, down_s, dhid_s, dproj_s, dmid_s, cot_s,
):
    f32, bf16 = jnp.float32, jnp.bfloat16
    width, length, half = MODEL_WIDTH, x_ref.shape[1], HEAD_SIZE // 2
    part = width // 2
    heads, kv = QUERY_HEADS, KEY_VALUE_HEADS
    repeat = heads // kv
    scale = HEAD_SIZE**-0.5
    first_panel = (heads * HEAD_SIZE) // LANES

    def zero_panel(p):
        return w_ref[0, pl.ds(p * width, width), :]

    def zero_pair(p):
        return jnp.concatenate([zero_panel(p), zero_panel(p + 1)], axis=-1)

    gain_one, gain_two = gain_ref[0:1, :], gain_ref[1:2, :]
    x = x_ref[...].astype(f32).T
    cot_s[...] = cot_ref[...].astype(f32).T.astype(bf16)
    inv_attn = lax.rsqrt(jnp.mean(x * x, axis=-1, keepdims=True) + norm_eps)
    normed_attn = x * inv_attn
    hidden_attn = (normed_attn * gain_one).astype(bf16)

    seg_row = jnp.broadcast_to(seg_ref[...].astype(f32), (length, length))
    rows = lax.broadcasted_iota(jnp.int32, (length, length), 0)
    columns = lax.broadcasted_iota(jnp.int32, (length, length), 1)
    allowed = (seg_row == seg_row.T) & (rows >= columns)
    positions = jnp.sum(jnp.where(allowed, 1.0, 0.0), axis=-1, keepdims=True) - 1.0
    angles = positions * freq_ref[...]
    lane = lax.broadcasted_iota(jnp.int32, (length, LANES), 1)
    first = lane % HEAD_SIZE < half
    cosine, sine = jnp.cos(angles), jnp.sin(angles)
    sine = jnp.where(first, -sine, sine)

    def swap(u):
        return jnp.where(first, pltpu.roll(u, LANES - half, 1), pltpu.roll(u, half, 1))

    plain = {}
    panels = 12
    for p in range(first_panel, panels, 2):
        both = dot(hidden_attn, zero_pair(p), 1, 0)
        plain[p], plain[p + 1] = both[:, :LANES], both[:, LANES:]
    turned = {p: u * cosine + swap(u) * sine for p, u in plain.items()}

    def slot(source, s):
        at = s % 2 * HEAD_SIZE
        return source[s // 2][:, at : at + HEAD_SIZE].astype(bf16)

    mask = jnp.concatenate([allowed] * repeat, axis=0)
    saved = []
    for j in range(kv):
        queries = jnp.concatenate([slot(turned, heads + repeat * j + r) for r in range(repeat)], axis=0)
        keys, values = slot(turned, 2 * heads + j), slot(plain, 2 * heads + kv + j)
        scores = jnp.where(mask, dot(queries, keys, 1, 1) * scale, masked_value)
        peak = jnp.max(scores, axis=-1, keepdims=True)
        total = jnp.sum(jnp.exp(scores - peak), axis=-1, keepdims=True)
        probs = jnp.exp(scores - (peak + jnp.log(total)))
        probs_b = probs.astype(bf16)
        attended = dot(probs_b, values, 1, 0)
        for r in range(repeat):
            at = (repeat * j + r) * HEAD_SIZE
            att_s[:, at : at + HEAD_SIZE] = attended[r * length : (r + 1) * length].astype(bf16)
        saved.append((queries, keys, values, probs, probs_b))

    attended = att_s[...]
    for p in range(0, first_panel, 2):
        at = p * LANES
        mid_s[:, at : at + 2 * LANES] = dot(attended, zero_pair(p), 1, 0)
    at = first_panel * LANES
    mid_s[:, at:width] = dot(attended, zero_panel(first_panel), 1, 0)[:, : width - at]
    mid = x + mid_s[...]
    inv_ffn = lax.rsqrt(jnp.mean(mid * mid, axis=-1, keepdims=True) + norm_eps)
    normed_ffn = mid * inv_ffn
    hid_s[...] = (normed_ffn * gain_two).astype(bf16)
    mid_s[...] = mid
    down_s[...] = jnp.zeros_like(down_s)
    dhid_s[...] = jnp.zeros_like(dhid_s)

    def gateup_rows(p):
        return pl.ds(pl.multiple_of(p * part, part), part)

    def gateup_pair(p):
        sides = [
            jnp.concatenate([w_ref[1, gateup_rows(q), :], w_ref[2, gateup_rows(q), :]], axis=0)
            for q in (p, p + 1)
        ]
        return jnp.concatenate(sides, axis=-1)

    def store_gateup(p, value):
        value = value.astype(bf16)
        for q in range(2):
            columns = slice(q * LANES, (q + 1) * LANES)
            main_ref[1, gateup_rows(p + q), :] = value[:part, columns]
            main_ref[2, gateup_rows(p + q), :] = value[part:, columns]

    half_panels = FF // LANES

    def hidden_step(i, _):
        p = 2 * i
        hidden, cotangent = hid_s[...], cot_s[...]
        gate_w, up_w = gateup_pair(p), gateup_pair(p + half_panels)
        down_rows = [pl.ds(pl.multiple_of((p + q) * width, width), width) for q in range(2)]
        down_w = jnp.concatenate([w_ref[3, r, :] for r in down_rows], axis=-1)
        gate, upper = dot(hidden, gate_w, 1, 0), dot(hidden, up_w, 1, 0)
        d_act = dot(cotangent, down_w, 1, 0)
        sigmoid = jax.nn.sigmoid(gate)
        activation = (gate * sigmoid * upper).astype(bf16)
        d_gate = (d_act * upper * sigmoid * (1.0 + gate * (1.0 - sigmoid))).astype(bf16)
        d_upper = (d_act * gate * sigmoid).astype(bf16)
        down_s[...] += dot(activation, down_w, 1, 1)
        dhid_s[...] += dot(d_gate, gate_w, 1, 1) + dot(d_upper, up_w, 1, 1)
        store_gateup(p, dot(hidden, d_gate, 0, 0))
        store_gateup(p + half_panels, dot(hidden, d_upper, 0, 0))
        d_down = dot(cot_ref[...], activation, 1, 0).astype(bf16)
        for q in range(2):
            main_ref[3, down_rows[q], :] = d_down[:, q * LANES : (q + 1) * LANES]
        return 0

    lax.fori_loop(0, half_panels // 2, hidden_step, 0)
    mid = mid_s[...]
    normed_ffn = mid * inv_ffn
    out_ref[...] = (mid + down_s[...]).T.astype(bf16)
    d_hidden = dhid_s[...]
    gg_ref[1:2, :] = jnp.sum(d_hidden * normed_ffn, axis=0, keepdims=True)
    d_mid = cot_s[...].astype(f32) + norm_back(d_hidden, normed_ffn, inv_ffn, gain_two)
    dmid_s[...] = jnp.zeros_like(dmid_s)
    dmid_s[:, :width] = d_mid.astype(bf16)
    attended = att_s[...]
    d_attended = jnp.zeros((length, width), f32)
    for p in range(0, first_panel + 2, 2):
        at = p * LANES
        if p == first_panel:
            block = dmid_s[:, at : at + LANES]
            d_attended += dot(block, zero_panel(p), 1, 1)
        else:
            block = dmid_s[:, at : at + 2 * LANES]
            d_attended += dot(block, zero_pair(p), 1, 1)
        value = dot(attended, block, 0, 0)
        if p == first_panel:
            edge = value
        else:
            main_ref[0, pl.ds(p * width, width), :] = value[:, :LANES].astype(bf16)
            main_ref[0, pl.ds((p + 1) * width, width), :] = value[:, LANES:].astype(bf16)
    att_s[...] = d_attended.astype(bf16)

    dproj_s[...] = jnp.zeros_like(dproj_s)
    start = first_panel * 2
    for j in range(kv):
        queries, keys, values, probs, probs_b = saved[j]
        d_att = jnp.concatenate(
            [
                att_s[:, (repeat * j + r) * HEAD_SIZE : (repeat * j + r + 1) * HEAD_SIZE]
                for r in range(repeat)
            ],
            axis=0,
        )
        d_probs = dot(d_att, values, 1, 1)
        row_total = jnp.sum(probs * d_probs, axis=-1, keepdims=True)
        d_scores = (probs * (d_probs - row_total) * scale).astype(bf16)
        d_queries = dot(d_scores, keys, 1, 0)
        for r in range(repeat):
            at = (heads + repeat * j + r - start) * HEAD_SIZE
            dproj_s[:, at : at + HEAD_SIZE] = d_queries[r * length : (r + 1) * length]
        at = (2 * heads + j - start) * HEAD_SIZE
        dproj_s[:, at : at + HEAD_SIZE] = dot(d_scores, queries, 0, 0)
        at = (2 * heads + kv + j - start) * HEAD_SIZE
        dproj_s[:, at : at + HEAD_SIZE] = dot(probs_b, d_att, 0, 0)

    turned_lanes = (2 * heads + kv - start) * HEAD_SIZE
    d_hidden = jnp.zeros((length, width), f32)
    for p in range(first_panel, panels, 2):
        sides = []
        for q in (p, p + 1):
            at = (q - first_panel) * LANES
            raw = dproj_s[:, at : at + LANES]
            back = raw * cosine - swap(raw) * sine
            sides.append(jnp.where(lane + at < turned_lanes, back, raw).astype(bf16))
        both = jnp.concatenate(sides, axis=-1)
        d_hidden += dot(both, zero_pair(p), 1, 1)
        value = dot(hidden_attn, both, 0, 0)
        left = value[:, :LANES]
        if p == first_panel:
            left = left + edge
        main_ref[0, pl.ds(p * width, width), :] = left.astype(bf16)
        main_ref[0, pl.ds((p + 1) * width, width), :] = value[:, LANES:].astype(bf16)
    gg_ref[0:1, :] = jnp.sum(d_hidden * normed_attn, axis=0, keepdims=True)
    din_ref[...] = (d_mid + norm_back(d_hidden, normed_attn, inv_attn, gain_one)).T.astype(bf16)


def layer_panels(inputs, segment_row, cotangent, weights, gains):
    length = inputs.shape[0]
    half = HEAD_SIZE // 2
    f32, bf16 = jnp.float32, jnp.bfloat16
    freqs = theta_base ** (-2.0 * jnp.arange(half, dtype=f32) / HEAD_SIZE)
    freqs = jnp.tile(freqs, LANES // half)[None]
    full = (length, MODEL_WIDTH)
    kept = (QUERY_HEADS * HEAD_SIZE) // LANES * LANES
    outputs, d_inputs, main, gains = pl.pallas_call(
        layer_kernel,
        out_shape=(
            jax.ShapeDtypeStruct(full[::-1], bf16),
            jax.ShapeDtypeStruct(full[::-1], bf16),
            jax.ShapeDtypeStruct(weights.shape, bf16),
            jax.ShapeDtypeStruct((2, MODEL_WIDTH), f32),
        ),
        in_specs=vmem_specs(6),
        out_specs=tuple(vmem_specs(4)),
        scratch_shapes=[
            pltpu.VMEM(full, bf16),
            pltpu.VMEM(full, f32),
            pltpu.VMEM(full, bf16),
            pltpu.VMEM(full, f32),
            pltpu.VMEM(full, f32),
            pltpu.VMEM((length, FF - kept), f32),
            pltpu.VMEM((length, kept + LANES), bf16),
            pltpu.VMEM(full, bf16),
        ],
        compiler_params=pltpu.CompilerParams(vmem_limit_bytes=60 * 2**20),
        name="layer",
    )(inputs.T, segment_row[None], cotangent.T, weights, gains.astype(f32).reshape(2, MODEL_WIDTH), freqs)
    return (outputs.T, d_inputs.T, main, gains)


def columns_to_panels(matrix):
    return matrix.reshape(matrix.shape[0], -1, LANES).swapaxes(0, 1).reshape(-1, LANES)


def panels_to_columns(panels, rows):
    return panels.reshape(-1, rows, LANES).swapaxes(0, 1).reshape(rows, -1)


def block_to_panels(flat, group):
    inner = QUERY_HEADS * HEAD_SIZE
    qkv = inner + 2 * KEY_VALUE_HEADS * HEAD_SIZE
    cut = MODEL_WIDTH * qkv

    def joint(v):
        out, w = v[cut:].reshape(inner, MODEL_WIDTH), v[:cut].reshape(MODEL_WIDTH, qkv)
        return columns_to_panels(jnp.concatenate([out, w], axis=1))

    def gateup(v):
        return columns_to_panels(v.reshape(-1, 2 * FF))

    def down(v):
        return columns_to_panels(v.reshape(FF, MODEL_WIDTH).T)

    return lax.switch(group, [joint, gateup, gateup, down], flat)


def panels_to_block(panels, group):
    inner = QUERY_HEADS * HEAD_SIZE

    def joint(v):
        both = panels_to_columns(v, MODEL_WIDTH)
        return jnp.concatenate([both[:, MODEL_WIDTH:].reshape(-1), both[:, :MODEL_WIDTH].reshape(-1)])

    def gateup(v):
        return panels_to_columns(v, MODEL_WIDTH // 2).reshape(-1)

    def down(v):
        return panels_to_columns(v, MODEL_WIDTH).T.reshape(-1)

    return lax.switch(group, [joint, gateup, gateup, down], panels)


def on_device(inputs, segments, cotangent, params, moment_one, moment_two):
    groups = lax.axis_size("group")
    wides = lax.axis_size("wide")
    group = lax.axis_index("group")
    count = wides.bit_length() - 1
    share_len = params.shape[0]
    gain_len = 2 * MODEL_WIDTH
    extra = gain_len // groups
    block_len = share_len - extra
    block_rows = block_len // LANES
    piece_rows = -(-block_rows // wides)
    chunks = 6 if piece_rows % 96 == 0 else 2
    piece_rows = -(-piece_rows // (16 * chunks)) * 16 * chunks
    padding = piece_rows * wides - block_rows
    lead = (2,) * count
    slices = chunks
    if piece_rows % 288 == 0:
        chunks = 18

    def to_pieces(rows):
        rows = rows.reshape(-1, block_rows, LANES)
        if padding:
            rows = jnp.pad(rows, ((0, 0), (0, padding), (0, 0)))
        return rows.reshape((-1,) + lead + (piece_rows, LANES))

    def from_pieces(pieces):
        rows = pieces.reshape(-1, piece_rows * wides, LANES)[:, :block_rows]
        return rows.reshape(-1, LANES)

    rounded = params.astype(jnp.bfloat16)
    tail = jnp.pad(rounded[share_len - gain_len :], (0, 16 * LANES - gain_len)).reshape(16, LANES)
    tails = gather_tails(tail, groups, 0).reshape(groups, -1)[:, :gain_len]
    before = lax.dynamic_index_in_dim(tails, (group + groups - 1) % groups, keepdims=False)
    joined = jnp.concatenate([before, rounded])
    block = lax.dynamic_slice(joined, (gain_len - extra * group,), (block_len,))
    by_panels = groups == 4 and block_len == MODEL_WIDTH * FF and not padding
    flat_gains = tails[groups - 1]
    if by_panels:
        block = block_to_panels(block, group)
        gathered = gather_blocks(to_pieces(block)[0], groups, count, slices)
        outputs, d_inputs, main, gains = layer_panels(
            inputs[0],
            segments[0],
            cotangent[0],
            gathered.reshape(groups, block_rows, LANES),
            flat_gains,
        )
        gains = gains.reshape(-1)
    else:
        gathered = gather_blocks(to_pieces(block)[0], groups, count, slices)
        weights = unpack(from_pieces(gathered), flat_gains)
        outputs, d_inputs, main, gains = layer_row(inputs[0], segments[0], cotangent[0], weights)
    gains = gains.astype(jnp.bfloat16).astype(jnp.float32)
    gains = jnp.pad(gains, (0, 16 * LANES - gain_len)).reshape(16, LANES)
    summed_block, head, gains, square = sum_blocks(to_pieces(main), gains, groups, count, chunks)
    gains = gains.reshape(-1)[:gain_len].astype(jnp.bfloat16)
    if by_panels:
        flat_block = panels_to_block(from_pieces(summed_block), group)
        head = jnp.pad(flat_block[:gain_len], (0, 16 * LANES - gain_len)).reshape(16, LANES)
        heads = gather_tails(head, groups, 3).reshape(groups, -1)[:, :gain_len]
        head = lax.dynamic_index_in_dim(heads, (group + 1) % groups, keepdims=False)
    else:
        flat_block = from_pieces(summed_block).reshape(-1)
        head = head.reshape(-1)[:gain_len]
    head = jnp.where(group == groups - 1, gains, head)
    joined = jnp.concatenate([flat_block, head])
    summed = lax.dynamic_slice(joined, (extra * group,), (share_len,)).astype(jnp.float32)
    clip_factor = square[0, 0]
    flat_index = group * share_len + jnp.arange(share_len, dtype=jnp.int32)
    decay_mask = flat_index < share_len * groups - gain_len
    new_params, new_moment_one, new_moment_two = adam_update(
        summed, clip_factor, params, moment_one, moment_two, decay_mask
    )
    return (outputs[None], d_inputs[None], summed, new_params, new_moment_one, new_moment_two)


def solution(mesh):
    return jax.shard_map(
        on_device,
        mesh=mesh,
        in_specs=(
            P(("wide", "group"), None, None),
            P(("wide", "group"), None),
            P(("wide", "group"), None, None),
            P("group"),
            P("group"),
            P("group"),
        ),
        out_specs=(
            P(("wide", "group"), None, None),
            P(("wide", "group"), None, None),
            P("group"),
            P("group"),
            P("group"),
            P("group"),
        ),
        check_vma=False,
    )
```

```python
import functools
import math

import jax
import jax.numpy as jnp
from jax import lax
from jax.experimental import pallas as pl
from jax.experimental.pallas import tpu as pltpu
from jax.sharding import PartitionSpec as P

MESH = pl.DeviceIdType.MESH
LANES = 128

MODEL_WIDTH = 576
QUERY_HEADS = 9
KEY_VALUE_HEADS = 3
HEAD_SIZE = 64
FF = 1536


norm_eps = 1e-05
theta_base = 10000.0
masked_value = -1e30
beta_one = 0.9
beta_two = 0.95
bias_one = 0.19
bias_two = 0.0975
learn_rate = 0.03
decay_rate = 0.1
adam_eps = 1e-08
max_norm = 1.0


def contract(pattern, left_op, right_op):
    return jnp.einsum(pattern, left_op, right_op, preferred_element_type=jnp.float32)


def inner_rows(left_op, right_op):
    return lax.dot_general(
        left_op, right_op, (((0,), (0,)), ((), ())), preferred_element_type=jnp.float32
    )


def outer_column_count(left_op, right_op):
    return lax.dot_general(
        left_op, right_op, (((1,), (1,)), ((), ())), preferred_element_type=jnp.float32
    )


def unpack(main, gains):
    query_key_value_width = (QUERY_HEADS + 2 * KEY_VALUE_HEADS) * HEAD_SIZE
    shapes = [
        (MODEL_WIDTH, query_key_value_width),
        (QUERY_HEADS * HEAD_SIZE, MODEL_WIDTH),
        (MODEL_WIDTH, 2 * FF),
        (FF, MODEL_WIDTH),
    ]
    pieces = []
    offset = 0
    for piece_shape in shapes:
        extent = math.prod(piece_shape) // LANES
        pieces.append(main[offset : offset + extent].reshape(piece_shape))
        offset += extent
    return pieces + [gains[:MODEL_WIDTH], gains[MODEL_WIDTH:]]


def positions_of(segment_row):
    index_row = jnp.arange(segment_row.shape[0], dtype=jnp.int32)
    previous = jnp.concatenate([segment_row[:1] - 1, segment_row[:-1]])
    starts = jnp.where(segment_row != previous, index_row, jnp.zeros_like(index_row))
    return index_row - lax.cummax(starts, axis=0)


def rope_tables(positions):
    half_size = HEAD_SIZE // 2
    freqs = theta_base ** (-2.0 * jnp.arange(half_size, dtype=jnp.float32) / HEAD_SIZE)
    angles = positions.astype(jnp.float32)[:, None] * freqs[None, :]
    return (jnp.cos(angles)[:, None, :], jnp.sin(angles)[:, None, :])


def apply_rotation(vectors, cosine_lookup, sine_lookup):
    half_size = HEAD_SIZE // 2
    first_half = vectors[..., :half_size]
    second_half = vectors[..., half_size:]
    return jnp.concatenate(
        [
            first_half * cosine_lookup - second_half * sine_lookup,
            second_half * cosine_lookup + first_half * sine_lookup,
        ],
        axis=-1,
    )


def unrotate(vectors, cosine_lookup, sine_lookup):
    half_size = HEAD_SIZE // 2
    first_half = vectors[..., :half_size]
    second_half = vectors[..., half_size:]
    return jnp.concatenate(
        [
            first_half * cosine_lookup + second_half * sine_lookup,
            second_half * cosine_lookup - first_half * sine_lookup,
        ],
        axis=-1,
    )


def norm_back(d_hidden, normed, inverse, gain):
    d_normed = d_hidden * gain
    return inverse * (d_normed - normed * jnp.mean(d_normed * normed, axis=-1, keepdims=True))


def layer_row(inputs, segment_row, cotangent, weights):
    query_key_value_weight, output_weight, w_gateup, w_down, gain_attn, gain_ffn = weights
    sequence_length = inputs.shape[0]
    repeat_count = QUERY_HEADS // KEY_VALUE_HEADS
    scale_factor = HEAD_SIZE ** (-0.5)
    gain_one = gain_attn.astype(jnp.float32)
    gain_two = gain_ffn.astype(jnp.float32)
    resid_in = inputs.astype(jnp.float32)
    inv_attn = lax.rsqrt(jnp.mean(resid_in * resid_in, axis=-1, keepdims=True) + norm_eps)
    normed_attn = resid_in * inv_attn
    hidden_attn = (normed_attn * gain_one).astype(jnp.bfloat16)
    projected_output = jnp.dot(
        hidden_attn, query_key_value_weight, preferred_element_type=jnp.float32
    )
    cosine_lookup, sine_lookup = rope_tables(positions_of(segment_row))
    query_rows = projected_output[:, : QUERY_HEADS * HEAD_SIZE].reshape(
        sequence_length, QUERY_HEADS, HEAD_SIZE
    )
    key_matrix = projected_output[
        :, QUERY_HEADS * HEAD_SIZE : (QUERY_HEADS + KEY_VALUE_HEADS) * HEAD_SIZE
    ].reshape(sequence_length, KEY_VALUE_HEADS, HEAD_SIZE)
    query_rows_rotated = (
        apply_rotation(query_rows, cosine_lookup, sine_lookup)
        .astype(jnp.bfloat16)
        .reshape(sequence_length, KEY_VALUE_HEADS, repeat_count, HEAD_SIZE)
    )
    keys_rot = apply_rotation(key_matrix, cosine_lookup, sine_lookup).astype(jnp.bfloat16)
    value_rows = (
        projected_output[:, (QUERY_HEADS + KEY_VALUE_HEADS) * HEAD_SIZE :]
        .reshape(sequence_length, KEY_VALUE_HEADS, HEAD_SIZE)
        .astype(jnp.bfloat16)
    )
    index_row = jnp.arange(sequence_length)
    allowed = (segment_row[:, None] == segment_row[None, :]) & (
        index_row[:, None] >= index_row[None, :]
    )
    scores = contract("qgrd,kgd->grqk", query_rows_rotated, keys_rot) * scale_factor
    scores = jnp.where(allowed, scores, masked_value)
    peak = jnp.max(scores, axis=-1, keepdims=True)
    log_total = peak + jnp.log(jnp.sum(jnp.exp(scores - peak), axis=-1, keepdims=True))
    probs_b = jnp.exp(scores - log_total).astype(jnp.bfloat16)
    attended = (
        contract("grqk,kgd->qgrd", probs_b, value_rows)
        .astype(jnp.bfloat16)
        .reshape(sequence_length, QUERY_HEADS * HEAD_SIZE)
    )
    mid = resid_in + jnp.dot(attended, output_weight, preferred_element_type=jnp.float32)
    inv_ffn = lax.rsqrt(jnp.mean(mid * mid, axis=-1, keepdims=True) + norm_eps)
    normed_ffn = mid * inv_ffn
    hidden_ffn = (normed_ffn * gain_two).astype(jnp.bfloat16)
    gate_up = jnp.dot(hidden_ffn, w_gateup, preferred_element_type=jnp.float32)
    gate_pre = gate_up[:, :FF]
    upper = gate_up[:, FF:]
    sigmoid_gate = jax.nn.sigmoid(gate_pre)
    activation = (gate_pre * sigmoid_gate * upper).astype(jnp.bfloat16)
    outputs = (mid + jnp.dot(activation, w_down, preferred_element_type=jnp.float32)).astype(
        jnp.bfloat16
    )
    grad_down = inner_rows(activation, cotangent)
    d_act = outer_column_count(cotangent, w_down)
    d_gate = d_act * upper * sigmoid_gate * (1.0 + gate_pre * (1.0 - sigmoid_gate))
    d_upper = d_act * gate_pre * sigmoid_gate
    d_gate_up = jnp.concatenate([d_gate, d_upper], axis=-1).astype(jnp.bfloat16)
    grad_gateup = inner_rows(hidden_ffn, d_gate_up)
    d_hidden_ffn = outer_column_count(d_gate_up, w_gateup)
    grad_gain_ffn = jnp.sum(d_hidden_ffn * normed_ffn, axis=0)
    d_mid = cotangent.astype(jnp.float32) + norm_back(d_hidden_ffn, normed_ffn, inv_ffn, gain_two)
    grad_middle_batch = d_mid.astype(jnp.bfloat16)
    grad_out = inner_rows(attended, grad_middle_batch)
    grad_attended_rows = (
        outer_column_count(grad_middle_batch, output_weight)
        .astype(jnp.bfloat16)
        .reshape(sequence_length, KEY_VALUE_HEADS, repeat_count, HEAD_SIZE)
    )
    recomputed = contract("qgrd,kgd->grqk", query_rows_rotated, keys_rot) * scale_factor
    probs = jnp.exp(jnp.where(allowed, recomputed, masked_value) - log_total)
    d_probs = contract("qgrd,kgd->grqk", grad_attended_rows, value_rows)
    row_total = jnp.sum(probs * d_probs, axis=-1, keepdims=True)
    d_scores = (probs * (d_probs - row_total) * scale_factor).astype(jnp.bfloat16)
    grad_query_rows = contract("grqk,kgd->qgrd", d_scores, keys_rot).reshape(
        sequence_length, QUERY_HEADS, HEAD_SIZE
    )
    grad_key_rows = contract("grqk,qgrd->kgd", d_scores, query_rows_rotated)
    grad_value_rows = contract("grqk,qgrd->kgd", probs_b, grad_attended_rows)
    grad_query_rows = unrotate(grad_query_rows, cosine_lookup, sine_lookup)
    grad_key_rows = unrotate(grad_key_rows, cosine_lookup, sine_lookup)
    grad_projected_rows = jnp.concatenate(
        [
            grad_query_rows.reshape(sequence_length, QUERY_HEADS * HEAD_SIZE),
            grad_key_rows.reshape(sequence_length, KEY_VALUE_HEADS * HEAD_SIZE),
            grad_value_rows.reshape(sequence_length, KEY_VALUE_HEADS * HEAD_SIZE),
        ],
        axis=-1,
    ).astype(jnp.bfloat16)
    grad_qkv = inner_rows(hidden_attn, grad_projected_rows)
    d_hidden_attn = outer_column_count(grad_projected_rows, query_key_value_weight)
    grad_gain_attn = jnp.sum(d_hidden_attn * normed_attn, axis=0)
    d_inputs = (d_mid + norm_back(d_hidden_attn, normed_attn, inv_attn, gain_one)).astype(
        jnp.bfloat16
    )
    matrices = [grad_qkv, grad_out, grad_gateup, grad_down]
    main = jnp.concatenate([m.astype(jnp.bfloat16).reshape(-1, LANES) for m in matrices])
    gains = jnp.concatenate([grad_gain_attn, grad_gain_ffn])
    return (outputs, d_inputs, main, gains)


def adam_update(grads, clip_factor, params, moment_one, moment_two, decay_mask):
    clipped = grads * clip_factor
    new_moment_one = beta_one * moment_one + (1.0 - beta_one) * clipped
    new_moment_two = beta_two * moment_two + (1.0 - beta_two) * clipped * clipped
    step_size = new_moment_one / bias_one / (jnp.sqrt(new_moment_two / bias_two) + adam_eps)
    decay_term = jnp.where(decay_mask, decay_rate * params, jnp.zeros_like(params))
    new_params = params - learn_rate * (step_size + decay_term)
    return (new_params, new_moment_one, new_moment_two)


def my_bits(wide, count):
    return [(wide // 2**b) % 2 for b in range(count)]


def flipped(wide, bit, b):
    return wide + (1 - 2 * bit) * 2**b


def greet(wide, group, bits, groups):
    barrier = pltpu.get_barrier_semaphore()
    peers = [(flipped(wide, bit, b), group) for b, bit in enumerate(bits)]
    peers += [(wide, (group + d) % groups) for d in range(1, groups)]
    for peer in peers:
        pl.semaphore_signal(barrier, inc=1, device_id=peer, device_id_type=MESH)
    pl.semaphore_wait(barrier, len(peers))


def send(src, dst, send_sem, recv_sem, peer):
    copy = pltpu.make_async_remote_copy(
        src_ref=src,
        dst_ref=dst,
        send_sem=send_sem,
        recv_sem=recv_sem,
        device_id=peer,
        device_id_type=MESH,
    )
    copy.start()
    return copy


def bit_order(chunk, count):
    rest = list(range(1, count))
    return [0] + (rest if chunk % 2 == 0 else rest[::-1])


def tails_kernel(groups, bits_count, tail_ref, out_ref, send_sem, recv_sem):
    wide, group = lax.axis_index("wide"), lax.axis_index("group")
    greet(wide, group, [], groups)
    out_ref[pl.ds(group, 1)] = tail_ref[...][None]
    copies = []
    for d in range(1, groups):
        copies.append(
            send(
                tail_ref,
                out_ref.at[group],
                send_sem.at[d - 1],
                recv_sem.at[d - 1],
                (wide, (group + d) % groups),
            )
        )
    for copy in copies:
        copy.wait()


def gather_kernel(groups, count, chunks, block_ref, out_ref, own_sem, zs, zr, ws, wr):
    wide, group = lax.axis_index("wide"), lax.axis_index("group")
    bits = my_bits(wide, count)
    step = block_ref.shape[-2] // chunks
    greet(wide, group, bits, groups)

    def place(ref, lead, open_bits, chunk):
        index = [slice(None) if b in open_bits else bits[b] for b in reversed(range(count))]
        return ref.at[tuple(lead + index + [pl.ds(chunk * step, step)])]

    def copy(src, dst, send_sem, recv_sem, peer):
        return pltpu.make_async_remote_copy(
            src_ref=src,
            dst_ref=dst,
            send_sem=send_sem,
            recv_sem=recv_sem,
            device_id=peer,
            device_id_type=MESH,
        )

    def along(way, d, c):
        source = (group - way * (d - 1) + groups) % groups
        unit = (0 if way > 0 else groups - 1) + d - 1
        src = place(block_ref, [], [], c) if d == 1 else place(out_ref, [source], [], c)
        return copy(
            src,
            place(out_ref, [source], [], c),
            zs.at[unit, c],
            zr.at[unit, c],
            (wide, (group + way + groups) % groups),
        )

    def passes(way, d):
        ahead = group + way
        behind = group - way * (d - 1)
        return (ahead >= 0) & (ahead < groups) & (behind >= 0) & (behind < groups)

    def comes(way, d):
        behind = group - way * d
        return (behind >= 0) & (behind < groups)

    def across(way, d, c, stage):
        order = bit_order(c, count)[::-1]
        b = order[stage]
        source = (group - way * d + groups) % groups
        unit = (0 if way > 0 else groups - 1) + d - 1
        here = place(out_ref, [source], order[:stage], c)
        return copy(
            here,
            here,
            ws.at[unit, c, stage],
            wr.at[unit, c, stage],
            (flipped(wide, bits[b], b), group),
        )

    units = [(d, c) for d in range(1, groups) for c in range(chunks)]
    for c in range(chunks):
        for way in (1, -1):

            @pl.when(passes(way, 1))
            def _():
                along(way, 1, c).start()

    own = pltpu.make_async_copy(block_ref, out_ref.at[group], own_sem)
    own.start()
    for tick in range(len(units) // 2 + count + 1):
        for u, (d, c) in reversed(list(enumerate(units))):
            stage = tick - u // 2
            if not 0 <= stage <= count:
                continue
            for way in (1, -1):

                @pl.when(comes(way, d))
                def _():
                    if stage == 0:
                        along(way, d, c).wait_recv()
                    else:
                        across(way, d, c, stage - 1).wait_recv()
                    if stage < count:
                        across(way, d, c, stage).start()

                if stage == 0 and d + 1 < groups:

                    @pl.when(passes(way, d + 1))
                    def _():
                        along(way, d + 1, c).start()

    for way in (1, -1):
        for d, c in units:

            @pl.when(passes(way, d))
            def _():
                along(way, d, c).wait_send()

            @pl.when(comes(way, d))
            def _():
                for stage in range(count):
                    across(way, d, c, stage).wait_send()

    own.wait()


def sum_kernel(groups, count, chunks, x_ref, gain_ref, out_ref, head_ref, gsum_ref, sq_ref, *scratch):
    recvs, accs = scratch[:count], scratch[count : 2 * count]
    recv_z, gain_w, gain_z, sq_z, piece_head = scratch[2 * count : 2 * count + 5]
    ss, sr, zs, zr, gs, gr, xs, xr, gzs, gzr, qs, qr, hs, hr = scratch[2 * count + 5 :]
    wide, group = lax.axis_index("wide"), lax.axis_index("group")
    bits = my_bits(wide, count)
    step = x_ref.shape[-2] // chunks
    greet(wide, group, bits, groups)
    copies = {}
    f32 = jnp.float32

    def partner(b):
        return (flipped(wide, bits[b], b), group)

    def part(c, stage, value):
        order = bit_order(c, count)
        left = sorted(order[stage:], reverse=True)
        return [value if b == order[stage] else slice(None) for b in left]

    def held(c, stage):
        return x_ref if stage == 0 else accs[stage - 1].at[c]

    def view(c, stage, flip):
        b = bit_order(c, count)[stage]
        index = [slice(None)] + part(c, stage, 1 - bits[b] if flip else bits[b])
        if stage == 0:
            index += [slice(None)] * (count + 2 - len(index) - 1)
            return x_ref.at[tuple(index + [pl.ds(c * step, step)])]
        return accs[stage - 1].at[tuple([c] + index)]

    def start_scatter(c, stage):
        b = bit_order(c, count)[stage]
        copies["s", c, stage] = send(
            view(c, stage, True), recvs[stage].at[c], ss.at[c, stage], sr.at[c, stage], partner(b)
        )

    def add_scatter(c, stage):
        copies["s", c, stage].wait_recv()
        mine, other, total = view(c, stage, False), recvs[stage].at[c], accs[stage].at[c]

        def body(i, _):
            total[i] = (mine[i].astype(f32) + other[i].astype(f32)).astype(jnp.bfloat16)
            return 0

        lax.fori_loop(0, groups, body, 0)

    def start_groups(c):
        for d in range(1, groups):
            to = (group + d) % groups
            copies["z", c, d] = send(
                accs[-1].at[c, to],
                recv_z.at[c, d - 1],
                zs.at[c, d - 1],
                zr.at[c, d - 1],
                (wide, to),
            )

    def place(open_bits, c):
        index = [slice(None) if b in open_bits else bits[b] for b in reversed(range(count))]
        return out_ref.at[tuple(index + [pl.ds(c * step, step)])]

    def add_groups(c):
        total = accs[-1][c, group].astype(f32)
        for d in range(1, groups):
            copies["z", c, d].wait_recv()
            total = total + recv_z[c, d - 1].astype(f32)
        place([], c)[...] = total.astype(jnp.bfloat16)

    def start_gather(c, stage):
        order = bit_order(c, count)[::-1]
        here = place(order[:stage], c)
        copies["g", c, stage] = send(
            here, here, gs.at[c, stage], gr.at[c, stage], partner(order[stage])
        )

    for c in range(chunks):
        start_scatter(c, 0)
    gain_w[0] = gain_ref[...]
    copies["x", 0] = send(gain_w.at[0], gain_w.at[count + 1], xs.at[0], xr.at[0], partner(0))

    for tick in range(chunks // 2 + 2 * count + 1):
        for c in reversed(range(chunks)):
            s = tick - c // 2
            if 0 <= s < count:
                add_scatter(c, s)
                if s + 1 < count:
                    start_scatter(c, s + 1)
                else:
                    start_groups(c)
            elif s == count:
                add_groups(c)
                start_gather(c, 0)
            elif count < s <= 2 * count:
                copies["g", c, s - count - 1].wait_recv()
                if s < 2 * count:
                    start_gather(c, s - count)
        if tick < count:
            copies["x", tick].wait_recv()
            gain_w[tick + 1] = gain_w[tick] + gain_w[count + 1 + tick]
            if tick + 1 < count:
                copies["x", tick + 1] = send(
                    gain_w.at[tick + 1],
                    gain_w.at[count + 2 + tick],
                    xs.at[tick + 1],
                    xr.at[tick + 1],
                    partner(tick + 1),
                )
            else:
                gain_z[pl.ds(group, 1)] = gain_w[pl.ds(count, 1)]
                for d in range(1, groups):
                    copies["gz", d] = send(
                        gain_w.at[count],
                        gain_z.at[group],
                        gzs.at[d - 1],
                        gzr.at[d - 1],
                        (wide, (group + d) % groups),
                    )

    first = tuple([0] * count + [pl.ds(0, 16)])
    copies["h"] = send(out_ref.at[first], head_ref, hs, hr, (wide, (group + groups - 1) % groups))
    flat_lead = out_ref.shape[:-2]

    def squares(i, total):
        index = tuple((i // 2**b) % 2 for b in reversed(range(len(flat_lead))))
        value = out_ref[index].astype(f32)
        value = value * value
        return total + jnp.sum(value.reshape(-1, 8, LANES), axis=0)

    square = lax.fori_loop(0, math.prod(flat_lead), squares, jnp.zeros((8, LANES), f32))
    piece_head[...] = square
    sq_z[pl.ds(group, 1)] = square[None]
    for d in range(1, groups):
        copies["q", d] = send(
            piece_head, sq_z.at[group], qs.at[d - 1], qr.at[d - 1], (wide, (group + d) % groups)
        )
    for d in range(1, groups):
        copies["gz", d].wait_recv()
    gains = gain_z[0]
    for d in range(1, groups):
        gains = gains + gain_z[d]
    gains = gains.astype(jnp.bfloat16).astype(f32)
    gsum_ref[...] = gains
    for d in range(1, groups):
        copies["q", d].wait_recv()
    square = sq_z[0]
    for d in range(1, groups):
        square = square + sq_z[d]
    square = square + jnp.sum((gains * gains).reshape(-1, 8, LANES), axis=0)
    total = jnp.sum(jnp.sum(square, axis=-1, keepdims=True), axis=0, keepdims=True)
    clip = jnp.minimum(jnp.float32(1.0), max_norm * lax.rsqrt(total))
    sq_ref[...] = jnp.broadcast_to(clip, sq_ref.shape)
    copies["h"].wait_recv()
    for copy in copies.values():
        copy.wait_send()


def params_of(identity):
    return pltpu.CompilerParams(
        collective_id=identity, has_side_effects=True, vmem_limit_bytes=60 * 2**20
    )


def vmem_specs(n):
    return [pl.BlockSpec(memory_space=pltpu.VMEM)] * n


def gather_tails(tail, groups, identity):
    dma = pltpu.SemaphoreType.DMA
    return pl.pallas_call(
        functools.partial(tails_kernel, groups, 0),
        out_shape=jax.ShapeDtypeStruct((groups,) + tail.shape, tail.dtype),
        in_specs=vmem_specs(1),
        out_specs=vmem_specs(1)[0],
        scratch_shapes=[dma((groups - 1,)), dma((groups - 1,))],
        compiler_params=params_of(identity),
        name="tails",
    )(tail)


def gather_blocks(block, groups, count, chunks):
    dma = pltpu.SemaphoreType.DMA
    units = 2 * (groups - 1)
    return pl.pallas_call(
        functools.partial(gather_kernel, groups, count, chunks),
        out_shape=jax.ShapeDtypeStruct((groups,) + block.shape, block.dtype),
        in_specs=vmem_specs(1),
        out_specs=vmem_specs(1)[0],
        scratch_shapes=[
            dma,
            dma((units, chunks)),
            dma((units, chunks)),
            dma((units, chunks, count)),
            dma((units, chunks, count)),
        ],
        compiler_params=params_of(1),
        name="gather_weights",
    )(block)


def sum_blocks(main, gains, groups, count, chunks):
    dma = pltpu.SemaphoreType.DMA
    rows = main.shape[-2]
    step = rows // chunks
    bf16, f32 = jnp.bfloat16, jnp.float32
    stages = [
        pltpu.VMEM((chunks, groups) + (2,) * (count - 1 - k) + (step, LANES), bf16)
        for k in range(count)
    ]
    return pl.pallas_call(
        functools.partial(sum_kernel, groups, count, chunks),
        out_shape=(
            jax.ShapeDtypeStruct((2,) * count + (rows, LANES), bf16),
            jax.ShapeDtypeStruct((16, LANES), bf16),
            jax.ShapeDtypeStruct(gains.shape, f32),
            jax.ShapeDtypeStruct((8, LANES), f32),
        ),
        in_specs=vmem_specs(2),
        out_specs=tuple(vmem_specs(4)),
        scratch_shapes=stages
        + stages
        + [
            pltpu.VMEM((chunks, groups - 1, step, LANES), bf16),
            pltpu.VMEM((2 * count + 1,) + gains.shape, f32),
            pltpu.VMEM((groups,) + gains.shape, f32),
            pltpu.VMEM((groups, 8, LANES), f32),
            pltpu.VMEM((8, LANES), f32),
        ]
        + [dma((chunks, count))] * 2
        + [dma((chunks, groups - 1))] * 2
        + [dma((chunks, count))] * 2
        + [dma((count,))] * 2
        + [dma((groups - 1,))] * 4
        + [dma, dma],
        compiler_params=params_of(2),
        name="sum_grads",
    )(main, gains)


def dot(left_op, right_op, left_dim, right_dim):
    return lax.dot_general(
        left_op,
        right_op,
        (((left_dim,), (right_dim,)), ((), ())),
        preferred_element_type=jnp.float32,
    )


def layer_kernel(
    x_ref, seg_ref, cot_ref, w_ref, gain_ref, freq_ref,
    out_ref, din_ref, main_ref, gg_ref,
    att_s, mid_s, hid_s, down_s, dhid_s, dproj_s, dmid_s, cot_s,
):
    f32, bf16 = jnp.float32, jnp.bfloat16
    width, length, half = MODEL_WIDTH, x_ref.shape[1], HEAD_SIZE // 2
    part = width // 2
    heads, kv = QUERY_HEADS, KEY_VALUE_HEADS
    repeat = heads // kv
    scale = HEAD_SIZE**-0.5
    first_panel = (heads * HEAD_SIZE) // LANES

    def zero_panel(p):
        return w_ref[0, pl.ds(p * width, width), :]

    def zero_pair(p):
        return jnp.concatenate([zero_panel(p), zero_panel(p + 1)], axis=-1)

    gain_one, gain_two = gain_ref[0:1, :], gain_ref[1:2, :]
    x = x_ref[...].astype(f32).T
    cot_s[...] = cot_ref[...].astype(f32).T.astype(bf16)
    inv_attn = lax.rsqrt(jnp.mean(x * x, axis=-1, keepdims=True) + norm_eps)
    normed_attn = x * inv_attn
    hidden_attn = (normed_attn * gain_one).astype(bf16)

    seg_row = jnp.broadcast_to(seg_ref[...].astype(f32), (length, length))
    rows = lax.broadcasted_iota(jnp.int32, (length, length), 0)
    columns = lax.broadcasted_iota(jnp.int32, (length, length), 1)
    allowed = (seg_row == seg_row.T) & (rows >= columns)
    positions = jnp.sum(jnp.where(allowed, 1.0, 0.0), axis=-1, keepdims=True) - 1.0
    angles = positions * freq_ref[...]
    lane = lax.broadcasted_iota(jnp.int32, (length, LANES), 1)
    first = lane % HEAD_SIZE < half
    cosine, sine = jnp.cos(angles), jnp.sin(angles)
    sine = jnp.where(first, -sine, sine)

    def swap(u):
        return jnp.where(first, pltpu.roll(u, LANES - half, 1), pltpu.roll(u, half, 1))

    plain = {}
    panels = 12
    for p in range(first_panel, panels, 2):
        both = dot(hidden_attn, zero_pair(p), 1, 0)
        plain[p], plain[p + 1] = both[:, :LANES], both[:, LANES:]
    turned = {p: u * cosine + swap(u) * sine for p, u in plain.items()}

    def slot(source, s):
        at = s % 2 * HEAD_SIZE
        return source[s // 2][:, at : at + HEAD_SIZE].astype(bf16)

    mask = jnp.concatenate([allowed] * repeat, axis=0)
    saved = []
    for j in range(kv):
        queries = jnp.concatenate([slot(turned, heads + repeat * j + r) for r in range(repeat)], axis=0)
        keys, values = slot(turned, 2 * heads + j), slot(plain, 2 * heads + kv + j)
        scores = jnp.where(mask, dot(queries, keys, 1, 1) * scale, masked_value)
        peak = jnp.max(scores, axis=-1, keepdims=True)
        total = jnp.sum(jnp.exp(scores - peak), axis=-1, keepdims=True)
        probs = jnp.exp(scores - (peak + jnp.log(total)))
        probs_b = probs.astype(bf16)
        attended = dot(probs_b, values, 1, 0)
        for r in range(repeat):
            at = (repeat * j + r) * HEAD_SIZE
            att_s[:, at : at + HEAD_SIZE] = attended[r * length : (r + 1) * length].astype(bf16)
        saved.append((queries, keys, values, probs, probs_b))

    attended = att_s[...]
    for p in range(0, first_panel, 2):
        at = p * LANES
        mid_s[:, at : at + 2 * LANES] = dot(attended, zero_pair(p), 1, 0)
    at = first_panel * LANES
    mid_s[:, at:width] = dot(attended, zero_panel(first_panel), 1, 0)[:, : width - at]
    mid = x + mid_s[...]
    inv_ffn = lax.rsqrt(jnp.mean(mid * mid, axis=-1, keepdims=True) + norm_eps)
    normed_ffn = mid * inv_ffn
    hid_s[...] = (normed_ffn * gain_two).astype(bf16)
    mid_s[...] = mid
    down_s[...] = jnp.zeros_like(down_s)
    dhid_s[...] = jnp.zeros_like(dhid_s)

    def gateup_rows(p):
        return pl.ds(pl.multiple_of(p * part, part), part)

    def gateup_pair(p):
        sides = [
            jnp.concatenate([w_ref[1, gateup_rows(q), :], w_ref[2, gateup_rows(q), :]], axis=0)
            for q in (p, p + 1)
        ]
        return jnp.concatenate(sides, axis=-1)

    def store_gateup(p, value):
        value = value.astype(bf16)
        for q in range(2):
            columns = slice(q * LANES, (q + 1) * LANES)
            main_ref[1, gateup_rows(p + q), :] = value[:part, columns]
            main_ref[2, gateup_rows(p + q), :] = value[part:, columns]

    half_panels = FF // LANES

    def hidden_step(i, _):
        p = 2 * i
        hidden, cotangent = hid_s[...], cot_s[...]
        gate_w, up_w = gateup_pair(p), gateup_pair(p + half_panels)
        down_rows = [pl.ds(pl.multiple_of((p + q) * width, width), width) for q in range(2)]
        down_w = jnp.concatenate([w_ref[3, r, :] for r in down_rows], axis=-1)
        gate, upper = dot(hidden, gate_w, 1, 0), dot(hidden, up_w, 1, 0)
        d_act = dot(cotangent, down_w, 1, 0)
        sigmoid = jax.nn.sigmoid(gate)
        activation = (gate * sigmoid * upper).astype(bf16)
        d_gate = (d_act * upper * sigmoid * (1.0 + gate * (1.0 - sigmoid))).astype(bf16)
        d_upper = (d_act * gate * sigmoid).astype(bf16)
        down_s[...] += dot(activation, down_w, 1, 1)
        dhid_s[...] += dot(d_gate, gate_w, 1, 1) + dot(d_upper, up_w, 1, 1)
        store_gateup(p, dot(hidden, d_gate, 0, 0))
        store_gateup(p + half_panels, dot(hidden, d_upper, 0, 0))
        d_down = dot(cot_ref[...], activation, 1, 0).astype(bf16)
        for q in range(2):
            main_ref[3, down_rows[q], :] = d_down[:, q * LANES : (q + 1) * LANES]
        return 0

    lax.fori_loop(0, half_panels // 2, hidden_step, 0)
    mid = mid_s[...]
    normed_ffn = mid * inv_ffn
    out_ref[...] = (mid + down_s[...]).T.astype(bf16)
    d_hidden = dhid_s[...]
    gg_ref[1:2, :] = jnp.sum(d_hidden * normed_ffn, axis=0, keepdims=True)
    d_mid = cot_s[...].astype(f32) + norm_back(d_hidden, normed_ffn, inv_ffn, gain_two)
    dmid_s[...] = jnp.zeros_like(dmid_s)
    dmid_s[:, :width] = d_mid.astype(bf16)
    attended = att_s[...]
    d_attended = jnp.zeros((length, width), f32)
    for p in range(0, first_panel + 2, 2):
        at = p * LANES
        if p == first_panel:
            block = dmid_s[:, at : at + LANES]
            d_attended += dot(block, zero_panel(p), 1, 1)
        else:
            block = dmid_s[:, at : at + 2 * LANES]
            d_attended += dot(block, zero_pair(p), 1, 1)
        value = dot(attended, block, 0, 0)
        if p == first_panel:
            edge = value
        else:
            main_ref[0, pl.ds(p * width, width), :] = value[:, :LANES].astype(bf16)
            main_ref[0, pl.ds((p + 1) * width, width), :] = value[:, LANES:].astype(bf16)
    att_s[...] = d_attended.astype(bf16)

    dproj_s[...] = jnp.zeros_like(dproj_s)
    start = first_panel * 2
    for j in range(kv):
        queries, keys, values, probs, probs_b = saved[j]
        d_att = jnp.concatenate(
            [
                att_s[:, (repeat * j + r) * HEAD_SIZE : (repeat * j + r + 1) * HEAD_SIZE]
                for r in range(repeat)
            ],
            axis=0,
        )
        d_probs = dot(d_att, values, 1, 1)
        row_total = jnp.sum(probs * d_probs, axis=-1, keepdims=True)
        d_scores = (probs * (d_probs - row_total) * scale).astype(bf16)
        d_queries = dot(d_scores, keys, 1, 0)
        for r in range(repeat):
            at = (heads + repeat * j + r - start) * HEAD_SIZE
            dproj_s[:, at : at + HEAD_SIZE] = d_queries[r * length : (r + 1) * length]
        at = (2 * heads + j - start) * HEAD_SIZE
        dproj_s[:, at : at + HEAD_SIZE] = dot(d_scores, queries, 0, 0)
        at = (2 * heads + kv + j - start) * HEAD_SIZE
        dproj_s[:, at : at + HEAD_SIZE] = dot(probs_b, d_att, 0, 0)

    turned_lanes = (2 * heads + kv - start) * HEAD_SIZE
    d_hidden = jnp.zeros((length, width), f32)
    for p in range(first_panel, panels, 2):
        sides = []
        for q in (p, p + 1):
            at = (q - first_panel) * LANES
            raw = dproj_s[:, at : at + LANES]
            back = raw * cosine - swap(raw) * sine
            sides.append(jnp.where(lane + at < turned_lanes, back, raw).astype(bf16))
        both = jnp.concatenate(sides, axis=-1)
        d_hidden += dot(both, zero_pair(p), 1, 1)
        value = dot(hidden_attn, both, 0, 0)
        left = value[:, :LANES]
        if p == first_panel:
            left = left + edge
        main_ref[0, pl.ds(p * width, width), :] = left.astype(bf16)
        main_ref[0, pl.ds((p + 1) * width, width), :] = value[:, LANES:].astype(bf16)
    gg_ref[0:1, :] = jnp.sum(d_hidden * normed_attn, axis=0, keepdims=True)
    din_ref[...] = (d_mid + norm_back(d_hidden, normed_attn, inv_attn, gain_one)).T.astype(bf16)


def layer_panels(inputs, segment_row, cotangent, weights, gains):
    length = inputs.shape[0]
    half = HEAD_SIZE // 2
    f32, bf16 = jnp.float32, jnp.bfloat16
    freqs = theta_base ** (-2.0 * jnp.arange(half, dtype=f32) / HEAD_SIZE)
    freqs = jnp.tile(freqs, LANES // half)[None]
    full = (length, MODEL_WIDTH)
    kept = (QUERY_HEADS * HEAD_SIZE) // LANES * LANES
    outputs, d_inputs, main, gains = pl.pallas_call(
        layer_kernel,
        out_shape=(
            jax.ShapeDtypeStruct(full[::-1], bf16),
            jax.ShapeDtypeStruct(full[::-1], bf16),
            jax.ShapeDtypeStruct(weights.shape, bf16),
            jax.ShapeDtypeStruct((2, MODEL_WIDTH), f32),
        ),
        in_specs=vmem_specs(6),
        out_specs=tuple(vmem_specs(4)),
        scratch_shapes=[
            pltpu.VMEM(full, bf16),
            pltpu.VMEM(full, f32),
            pltpu.VMEM(full, bf16),
            pltpu.VMEM(full, f32),
            pltpu.VMEM(full, f32),
            pltpu.VMEM((length, FF - kept), f32),
            pltpu.VMEM((length, kept + LANES), bf16),
            pltpu.VMEM(full, bf16),
        ],
        compiler_params=pltpu.CompilerParams(vmem_limit_bytes=60 * 2**20),
        name="layer",
    )(inputs.T, segment_row[None], cotangent.T, weights, gains.astype(f32).reshape(2, MODEL_WIDTH), freqs)
    return (outputs.T, d_inputs.T, main, gains)


def columns_to_panels(matrix):
    return matrix.reshape(matrix.shape[0], -1, LANES).swapaxes(0, 1).reshape(-1, LANES)


def panels_to_columns(panels, rows):
    return panels.reshape(-1, rows, LANES).swapaxes(0, 1).reshape(rows, -1)


def block_to_panels(flat, group):
    inner = QUERY_HEADS * HEAD_SIZE
    qkv = inner + 2 * KEY_VALUE_HEADS * HEAD_SIZE
    cut = MODEL_WIDTH * qkv

    def joint(v):
        out, w = v[cut:].reshape(inner, MODEL_WIDTH), v[:cut].reshape(MODEL_WIDTH, qkv)
        return columns_to_panels(jnp.concatenate([out, w], axis=1))

    def gateup(v):
        return columns_to_panels(v.reshape(-1, 2 * FF))

    def down(v):
        return columns_to_panels(v.reshape(FF, MODEL_WIDTH).T)

    return lax.switch(group, [joint, gateup, gateup, down], flat)


def panels_to_block(panels, group):
    inner = QUERY_HEADS * HEAD_SIZE

    def joint(v):
        both = panels_to_columns(v, MODEL_WIDTH)
        return jnp.concatenate([both[:, MODEL_WIDTH:].reshape(-1), both[:, :MODEL_WIDTH].reshape(-1)])

    def gateup(v):
        return panels_to_columns(v, MODEL_WIDTH // 2).reshape(-1)

    def down(v):
        return panels_to_columns(v, MODEL_WIDTH).T.reshape(-1)

    return lax.switch(group, [joint, gateup, gateup, down], panels)


def on_device(inputs, segments, cotangent, params, moment_one, moment_two):
    groups = lax.axis_size("group")
    wides = lax.axis_size("wide")
    group = lax.axis_index("group")
    count = wides.bit_length() - 1
    share_len = params.shape[0]
    gain_len = 2 * MODEL_WIDTH
    extra = gain_len // groups
    block_len = share_len - extra
    block_rows = block_len // LANES
    piece_rows = -(-block_rows // wides)
    chunks = 6 if piece_rows % 96 == 0 else 2
    piece_rows = -(-piece_rows // (16 * chunks)) * 16 * chunks
    padding = piece_rows * wides - block_rows
    lead = (2,) * count

    def to_pieces(rows):
        rows = rows.reshape(-1, block_rows, LANES)
        if padding:
            rows = jnp.pad(rows, ((0, 0), (0, padding), (0, 0)))
        return rows.reshape((-1,) + lead + (piece_rows, LANES))

    def from_pieces(pieces):
        rows = pieces.reshape(-1, piece_rows * wides, LANES)[:, :block_rows]
        return rows.reshape(-1, LANES)

    rounded = params.astype(jnp.bfloat16)
    tail = jnp.pad(rounded[share_len - gain_len :], (0, 16 * LANES - gain_len)).reshape(16, LANES)
    tails = gather_tails(tail, groups, 0).reshape(groups, -1)[:, :gain_len]
    before = lax.dynamic_index_in_dim(tails, (group + groups - 1) % groups, keepdims=False)
    joined = jnp.concatenate([before, rounded])
    block = lax.dynamic_slice(joined, (gain_len - extra * group,), (block_len,))
    by_panels = groups == 4 and block_len == MODEL_WIDTH * FF and not padding
    flat_gains = tails[groups - 1]
    if by_panels:
        block = block_to_panels(block, group)
        gathered = gather_blocks(to_pieces(block)[0], groups, count, chunks)
        outputs, d_inputs, main, gains = layer_panels(
            inputs[0],
            segments[0],
            cotangent[0],
            gathered.reshape(groups, block_rows, LANES),
            flat_gains,
        )
        gains = gains.reshape(-1)
    else:
        gathered = gather_blocks(to_pieces(block)[0], groups, count, chunks)
        weights = unpack(from_pieces(gathered), flat_gains)
        outputs, d_inputs, main, gains = layer_row(inputs[0], segments[0], cotangent[0], weights)
    gains = gains.astype(jnp.bfloat16).astype(jnp.float32)
    gains = jnp.pad(gains, (0, 16 * LANES - gain_len)).reshape(16, LANES)
    summed_block, head, gains, square = sum_blocks(to_pieces(main), gains, groups, count, chunks)
    gains = gains.reshape(-1)[:gain_len].astype(jnp.bfloat16)
    if by_panels:
        flat_block = panels_to_block(from_pieces(summed_block), group)
        head = jnp.pad(flat_block[:gain_len], (0, 16 * LANES - gain_len)).reshape(16, LANES)
        heads = gather_tails(head, groups, 3).reshape(groups, -1)[:, :gain_len]
        head = lax.dynamic_index_in_dim(heads, (group + 1) % groups, keepdims=False)
    else:
        flat_block = from_pieces(summed_block).reshape(-1)
        head = head.reshape(-1)[:gain_len]
    head = jnp.where(group == groups - 1, gains, head)
    joined = jnp.concatenate([flat_block, head])
    summed = lax.dynamic_slice(joined, (extra * group,), (share_len,)).astype(jnp.float32)
    clip_factor = square[0, 0]
    flat_index = group * share_len + jnp.arange(share_len, dtype=jnp.int32)
    decay_mask = flat_index < share_len * groups - gain_len
    new_params, new_moment_one, new_moment_two = adam_update(
        summed, clip_factor, params, moment_one, moment_two, decay_mask
    )
    return (outputs[None], d_inputs[None], summed, new_params, new_moment_one, new_moment_two)


def solution(mesh):
    return jax.shard_map(
        on_device,
        mesh=mesh,
        in_specs=(
            P(("wide", "group"), None, None),
            P(("wide", "group"), None),
            P(("wide", "group"), None, None),
            P("group"),
            P("group"),
            P("group"),
        ),
        out_specs=(
            P(("wide", "group"), None, None),
            P(("wide", "group"), None, None),
            P("group"),
            P("group"),
            P("group"),
            P("group"),
        ),
        check_vma=False,
    )
```
